512 devices in a mesh: gx: 64 (over y, x, z_hi), ba: 8 (over z_lo, core).
Axes of the slice: x: 4, y: 8, z: 8 (z_hi: 2, z_lo: 4; z = z_hi * 4 + z_lo), core: 2. Of those that a mesh axis runs over, the one named last changes fastest.
Arguments:
- density: float32 [64, 128, 64, 128], P('ba', 'gx'), may hold values from 0.2 to 2
- diffusivity: float32 [64], P('ba'), may hold values from 0.03 to 0.16
- positions: int32 [512], replicated, may hold values from 0 to 1048575
- spectrum: float32 [512, 64], P(None, 'ba'), may hold values from 0.3 to 3
- cell_class: int32 [128, 64, 128], P('gx', 'ba'), may hold values from 0 to 63, as said below
- operators: bfloat16 [64, 64, 64], replicated, as said below
Outputs:
- updated: float32 [64, 128, 64, 128], P(None, 'gx', 'ba')
The draws below stay inside these ranges and needn't reach their ends.
Inputs may be any that keep to these rules, and one draw needn't show every extreme that they name: `cell_class`: among the cells of one device (x planes of one index of gx, y rows of one index of ba) no class appears more than 64 times, and on every device some class appears exactly 64 times. `operators`: each matrix has positive diagonal entries and full rank.
All inputs are finite; a program needn't handle non-finite values.
Results may differ from the reference program's by a relative error of at most 0.003.
Values may be sent and summed in bfloat16 or wider, within the bound.
A program may use at most 64 MiB of HBM per device.

```python
import math
import jax
import jax.numpy as jnp
from jax import lax

BINS = 64
CLASSES = 64
CX = 2
NY = 64
NZ = 128
REMNANTS = 512
NX = 128
N_GX = 64
N_BA = 8


def draw_cell_class(key, part):
    devices_all = N_GX * N_BA
    rows_y = NY // N_BA
    per_device = CX * rows_y * NZ
    block_count = per_device // CLASSES
    hot_class = jax.random.randint(jax.random.fold_in(key, 1), (devices_all,), 0, CLASSES)
    hot_block = jnp.repeat(hot_class, block_count)
    perm_keys = jax.random.split(jax.random.fold_in(key, 2), devices_all * block_count)
    others = jax.vmap(lambda single_key: jax.random.permutation(single_key, CLASSES - 1))(perm_keys)
    mapped = others + (others >= hot_block[:, None]).astype(jnp.int32)
    table = jnp.concatenate([hot_block[:, None], mapped], axis=1).astype(jnp.int32)
    choose_bits = jax.random.randint(jax.random.fold_in(key, 3), (devices_all * block_count, CLASSES), 0, 2)
    column = jnp.arange(CLASSES, dtype=jnp.int32)
    picked = column // 2 * 2 + choose_bits
    picked = jnp.where(column[None, :] < 2, 0, picked).astype(jnp.int32)
    classes = jnp.take_along_axis(table, picked, axis=1)
    classes = classes.reshape(N_GX, N_BA, CX, rows_y, NZ)
    classes = jnp.transpose(classes, (0, 2, 1, 3, 4))
    return classes.reshape(N_GX * CX, NY, NZ).astype(jnp.int32)


def draw_operators(key, part):
    diagonal_part = jax.random.uniform(jax.random.fold_in(key, 11), (CLASSES, BINS), jnp.float32, 0.5, 1.0)
    coupling = 0.4 * jax.random.normal(jax.random.fold_in(key, 12), (CLASSES, BINS, BINS), jnp.float32) / math.sqrt(BINS)
    identity = jnp.eye(BINS, dtype=jnp.float32)
    return (coupling * (1.0 - identity)[None] + identity[None] * diagonal_part[:, :, None]).astype(jnp.bfloat16)


def set_ends(result, own_key, smallest, top_value):
    extent = result.shape
    index_at = [jax.random.randint(jax.random.fold_in(own_key, axis), (), 0, extent[axis]) for axis in range(len(extent))]
    result = result.at[tuple(index_at)].set(smallest)
    longest = extent.index(max(extent))
    index_at[longest] = (index_at[longest] + 1) % extent[longest]
    return result.at[tuple(index_at)].set(top_value)


def shard_levels(stream_key, extent, cuts, low, top_value):
    gain, own = 1.0, jax.random.fold_in(stream_key, 6)
    for dim, shards_of in cuts:
        draws = jnp.exp(jax.random.uniform(jax.random.fold_in(own, dim), (shards_of,), jnp.float32, low / len(cuts), top_value / len(cuts)))
        gain = gain * jnp.repeat(draws, extent[dim] // shards_of).reshape([-1 if axis == dim else 1 for axis in range(len(extent))])
    return gain


def setup_inputs(seed: int = 0) -> dict:
    key_of = jax.random.split(jax.random.key(seed), 7)
    density = jnp.clip(0.2 + 1.8 * jax.random.uniform(key_of[0], (BINS, NX, NY, NZ), jnp.float32) ** shard_levels(key_of[0], (BINS, NX, NY, NZ), ((0, 8), (1, 64)), -0.2, 0.2), 0.2, 2.0)
    diffusivity = jnp.clip(jnp.exp(math.log(0.16) - 1.6739764 * jax.random.uniform(key_of[1], (BINS,), jnp.float32) ** shard_levels(key_of[1], (BINS,), ((0, 8),), -0.2, 0.2)), 0.03, 0.16)
    positions = set_ends(jax.random.randint(key_of[2], (REMNANTS,), 0, NX * NY * NZ), jax.random.fold_in(key_of[2], 1), 0, (NX * NY * NZ) - 1).astype(jnp.int32)
    spectrum = jnp.clip(jnp.exp(math.log(3.0) - 2.3025851 * jax.random.uniform(key_of[3], (REMNANTS, BINS), jnp.float32) ** shard_levels(key_of[3], (REMNANTS, BINS), ((1, 8),), -0.2, 0.2)), 0.3, 3.0)
    cell_class = draw_cell_class(jax.random.fold_in(key_of[6], 71), 0)
    operators = draw_operators(jax.random.fold_in(key_of[6], 71), 0)
    return dict(density=density, diffusivity=diffusivity, positions=positions, spectrum=spectrum, cell_class=cell_class, operators=operators)


def laplace(field):
    total_sum = -6.0 * field
    for axis_index in (1, 2, 3):
        total_sum = total_sum + jnp.roll(field, 1, axis_index) + jnp.roll(field, -1, axis_index)
    return total_sum


def reference(density, diffusivity, positions, spectrum, cell_class, operators):
    flat_source = jnp.zeros((BINS, NX * NY * NZ), jnp.float32)
    flat_source = flat_source.at[:, positions].add(spectrum.T.astype(jnp.float32))
    source = flat_source.reshape(BINS, NX, NY, NZ)
    diffusion = diffusivity[:, None, None, None]
    first_step = density + diffusion * laplace(density) + source
    second_step = first_step + diffusion * laplace(first_step) + source
    rounded = second_step.astype(jnp.bfloat16).reshape(BINS, NX * NY * NZ)
    classes = cell_class.reshape(-1)

    def apply_class(output, kind_index):
        product = jnp.dot(operators[kind_index], rounded, preferred_element_type=jnp.float32)
        return jnp.where(classes[None, :] == kind_index, product, output), None

    output, unused = lax.scan(apply_class, jnp.zeros((BINS, NX * NY * NZ), jnp.float32), jnp.arange(CLASSES, dtype=jnp.int32))
    return output.reshape(BINS, NX, NY, NZ)
```

```python
import functools

import jax
import jax.numpy as jnp
from jax import lax
from jax.experimental import pallas as pl
from jax.experimental.pallas import tpu as pltpu
from jax.sharding import PartitionSpec as P

MESH = pl.DeviceIdType.MESH

LOW = 0.1
STEPS = 32767.0
BIAS = 32768


def encode(rho):
    return ((rho - LOW) * STEPS + 0.5).astype(jnp.int32) - BIAS


def decode(code):
    return code.astype(jnp.int32).astype(jnp.float32) * (1.0 / STEPS) + (LOW + BIAS / STEPS)


def yz_sum(field):
    return (
        pltpu.roll(field, 1, 0)
        + pltpu.roll(field, field.shape[0] - 1, 0)
        + pltpu.roll(field, 1, 1)
        + pltpu.roll(field, field.shape[1] - 1, 1)
    )


def kernel(
    gx_count,
    ba_count,
    diff_ref,
    density_ref,
    pos_ref,
    spec_ref,
    class_ref,
    oper_ref,
    out_ref,
    dens,
    stage,
    held,
    halo,
    parm_out,
    parm,
    source,
    rounded,
    gathered,
    wide,
    opers,
    weights,
    load_sem,
    swap_send,
    swap_recv,
    parm_send,
    parm_recv,
    halo_send,
    halo_recv,
    spread_send,
    spread_recv,
):
    bins_dev, planes, rows_y, grid_z = density_ref.shape
    half = bins_dev // 2
    ring = 2 * ba_count
    rows_dev = rows_y // ba_count
    bins_all = gathered.shape[0]
    remnants = pos_ref.shape[1]
    part = remnants // 2
    gx = lax.axis_index("gx")
    ba = lax.axis_index("ba")
    side = lax.rem(gx, 2)
    column = gx - side
    me = side * ba_count + ba
    meet = lax.rem(ba + ba_count // 2, ba_count)
    right = lax.rem(gx + 2, gx_count)
    left = lax.rem(gx + gx_count - 2, gx_count)

    load_density = [
        pltpu.make_async_copy(
            density_ref.at[pl.ds(h * half, half)], dens.at[pl.ds(h * half, half)], load_sem.at[h]
        )
        for h in range(2)
    ]
    for copy in load_density:
        copy.start()
    load_opers = pltpu.make_async_copy(oper_ref, opers, load_sem.at[2])
    load_opers.start()

    barrier = pltpu.get_barrier_semaphore()
    for offset in range(1, ring):
        peer = lax.rem(me + offset, ring)
        pl.semaphore_signal(
            barrier,
            inc=1,
            device_id=(column + peer // ba_count, lax.rem(peer, ba_count)),
            device_id_type=MESH,
        )
    for other in (left, right):
        pl.semaphore_signal(barrier, inc=1, device_id=(other, ba), device_id_type=MESH)

    bin_row = lax.broadcasted_iota(jnp.int32, (half, grid_z), 0)
    for h in range(2):
        parm_out[h, :, 0:part] = spec_ref[
            h * half : (h + 1) * half, pl.ds(pl.multiple_of(side * part, part), part)
        ]
        value = jnp.zeros((half, grid_z), jnp.float32)
        for b in range(half):
            value = jnp.where(bin_row == b, diff_ref[h * half + b], value)
        parm_out[h, :, part:] = value
    for h in range(2):
        load_density[h].wait()
        for b in range(half):
            stage[h, b] = encode(dens[h * half + b]).astype(jnp.int16)

    pl.semaphore_wait(barrier, ring + 1)

    swaps = []
    parms = []
    for h in range(2):
        target = (column + h, meet)
        parms.append(
            pltpu.make_async_remote_copy(
                src_ref=parm_out.at[h],
                dst_ref=parm.at[side],
                send_sem=parm_send.at[h],
                recv_sem=parm_recv.at[side],
                device_id=target,
                device_id_type=MESH,
            )
        )
        parms[h].start()
    for b in range(half):
        for h in range(2):
            swaps.append(
                pltpu.make_async_remote_copy(
                    src_ref=stage.at[h, b],
                    dst_ref=held.at[side, b],
                    send_sem=swap_send.at[h, b],
                    recv_sem=swap_recv.at[side, b],
                    device_id=(column + h, meet),
                    device_id_type=MESH,
                )
            )
            swaps[-1].start()

    load_opers.wait()
    groups = weights.shape[0] // bins_all
    per_group = weights.shape[1] // bins_all

    def arrange(a, carry):
        weights[pl.ds(pl.multiple_of(a * bins_all, bins_all), bins_all), :] = jnp.concatenate(
            [opers[a * per_group + j] for j in range(per_group)], axis=1
        )
        return carry

    lax.fori_loop(0, groups, arrange, 0)

    def wait_parm(s):
        pltpu.make_async_copy(parm.at[s], parm.at[s], parm_recv.at[s]).wait()

    wait_parm(0)
    wait_parm(1)
    planes_col = 2 * planes
    planes_src = planes_col + 2
    pos = pos_ref[...]
    pos_x = pos // (rows_y * grid_z)
    pos_y = lax.rem(pos // grid_z, rows_y)
    pos_z = lax.rem(pos, grid_z)
    width = gx_count * planes
    pos_x = lax.rem(pos_x + (width + 1) - column * planes, width)
    pos_row = pos_x * rows_y + pos_y
    is_row = lax.broadcasted_iota(jnp.int32, (planes_src * rows_y, remnants), 0) == pos_row
    is_z = lax.broadcasted_iota(jnp.int32, (grid_z, remnants), 0) == pos_z
    is_z = jnp.where(is_z, 1.0, 0.0).astype(jnp.bfloat16)
    for b in range(half):
        spec = jnp.concatenate([parm[0, b : b + 1, 0:part], parm[1, b : b + 1, 0:part]], axis=1)
        high = spec.astype(jnp.bfloat16).astype(jnp.float32)
        low = spec - high
        total = jnp.zeros((planes_src * rows_y, grid_z), jnp.float32)
        for piece in (high, low):
            total += lax.dot_general(
                jnp.where(is_row, piece, 0.0).astype(jnp.bfloat16),
                is_z,
                (((1,), (1,)), ((), ())),
                preferred_element_type=jnp.float32,
            )
        source[b] = total.reshape(planes_src, rows_y, grid_z)

    halos = [[None, None] for _ in range(half)]

    def forward(b):
        for s in range(2):
            pltpu.make_async_copy(held.at[s, b], held.at[s, b], swap_recv.at[s, b]).wait()
            halos[b][s] = pltpu.make_async_remote_copy(
                src_ref=held.at[s, b],
                dst_ref=halo.at[s, b],
                send_sem=halo_send.at[s, b],
                recv_sem=halo_recv.at[s, b],
                device_id=(left if s == 0 else right, ba),
                device_id_type=MESH,
            )
            halos[b][s].start()

    def diffuse(b):
        for s in range(2):
            halos[b][s].wait_recv()
        rate = parm[0, b : b + 1, part:]
        centre = 1.0 - 6.0 * rate
        fields = [decode(halo[1, b, p]) for p in range(planes)]
        fields += [decode(held[s, b, p]) for s in range(2) for p in range(planes)]
        fields += [decode(halo[0, b, p]) for p in range(planes)]
        sources = [source[b, p] for p in range(planes_src)]
        first = [
            centre * fields[p + 1] + rate * (fields[p] + fields[p + 2] + yz_sum(fields[p + 1])) + sources[p]
            for p in range(planes_src)
        ]
        second = [
            centre * first[p + 1]
            + rate * (first[p] + first[p + 2] + yz_sum(first[p + 1]))
            + sources[p + 1]
            for p in range(planes_col)
        ]
        for s in range(2):
            block = jnp.concatenate(
                [second[s * planes + p].reshape(ba_count, rows_dev, grid_z) for p in range(planes)],
                axis=1,
            )
            rounded[b, pl.ds(s * ba_count, ba_count)] = block.astype(jnp.bfloat16)

    group = 2 * meet + side

    def spread(b):
        slot = gathered.at[group * half + b]
        for offset in list(range(ring // 2, ring)) + list(range(1, ring // 2)):
            peer = lax.rem(me + offset, ring)
            pltpu.make_async_remote_copy(
                src_ref=rounded.at[b, peer],
                dst_ref=slot,
                send_sem=spread_send,
                recv_sem=spread_recv,
                device_id=(column + peer // ba_count, lax.rem(peer, ba_count)),
                device_id_type=MESH,
            ).start()
        pltpu.make_async_copy(rounded.at[b, me], slot, spread_recv).start()

    forward(0)
    for b in range(half):
        if b + 1 < half:
            forward(b + 1)
        diffuse(b)
        spread(b)

    pltpu.make_async_copy(gathered, gathered, spread_recv).wait()

    wide[...] = gathered[...].astype(jnp.float32).reshape(wide.shape)
    cells = planes * rows_dev

    def update(step, carry):
        first_row = 2 * step
        values = jnp.concatenate(
            [wide[pl.ds(first_row + j, bins_all, stride=cells), :] for j in range(2)], axis=1
        )
        classes = jnp.concatenate([class_ref[pl.ds(first_row + j, 1), :] for j in range(2)], axis=1)
        within = lax.rem(classes, per_group)
        outer = classes // per_group
        stacked = jnp.concatenate(
            [jnp.where(within == j, values, 0.0) for j in range(per_group)], axis=0
        ).astype(jnp.bfloat16)
        products = jnp.dot(weights[...], stacked, preferred_element_type=jnp.float32)
        result = products[0:bins_all]
        for a in range(1, groups):
            result = jnp.where(outer == a, products[a * bins_all : (a + 1) * bins_all], result)
        for j in range(2):
            out_ref[pl.ds(first_row + j, bins_all, stride=cells), :] = result[
                :, j * grid_z : (j + 1) * grid_z
            ]
        return carry

    lax.fori_loop(0, cells // 2, update, 0)

    for copy in parms + swaps:
        copy.wait_send()
    for b in range(half):
        for s in range(2):
            halos[b][s].wait_send()
    sent = rounded.at[:, pl.ds(0, ring - 1)]
    pltpu.make_async_copy(sent, sent, spread_send).wait()


def solution(mesh):
    gx_count, ba_count = mesh.shape["gx"], mesh.shape["ba"]

    def step(density, diffusivity, positions, spectrum, cell_class, operators):
        bins_dev, planes, rows_y, grid_z = density.shape
        classes, bins_all, _ = operators.shape
        remnants = positions.shape[0]
        half = bins_dev // 2
        cells = planes * (rows_y // ba_count)
        per_group = 4
        vmem = pl.BlockSpec(memory_space=pltpu.VMEM)
        anywhere = pl.BlockSpec(memory_space=pl.ANY)
        out = pl.pallas_call(
            functools.partial(kernel, gx_count, ba_count),
            out_shape=jax.ShapeDtypeStruct((bins_all * cells, grid_z), jnp.float32),
            in_specs=[
                pl.BlockSpec(memory_space=pltpu.SMEM),
                anywhere,
                vmem,
                vmem,
                vmem,
                anywhere,
            ],
            out_specs=vmem,
            scratch_shapes=[
                pltpu.VMEM(density.shape, jnp.float32),
                pltpu.VMEM((2, half, planes, rows_y, grid_z), jnp.int16),
                pltpu.VMEM((2, half, planes, rows_y, grid_z), jnp.int16),
                pltpu.VMEM((2, half, planes, rows_y, grid_z), jnp.int16),
                pltpu.VMEM((2, half, remnants // 2 + grid_z), jnp.float32),
                pltpu.VMEM((2, half, remnants // 2 + grid_z), jnp.float32),
                pltpu.VMEM((half, 2 * planes + 2, rows_y, grid_z), jnp.float32),
                pltpu.VMEM((half, 2 * ba_count, cells, grid_z), jnp.bfloat16),
                pltpu.VMEM((bins_all, cells, grid_z), jnp.bfloat16),
                pltpu.VMEM((bins_all * cells, grid_z), jnp.float32),
                pltpu.VMEM(operators.shape, jnp.bfloat16),
                pltpu.VMEM((classes // per_group * bins_all, per_group * bins_all), jnp.bfloat16),
                pltpu.SemaphoreType.DMA((3,)),
                pltpu.SemaphoreType.DMA((2, half)),
                pltpu.SemaphoreType.DMA((2, half)),
                pltpu.SemaphoreType.DMA((2,)),
                pltpu.SemaphoreType.DMA((2,)),
                pltpu.SemaphoreType.DMA((2, half)),
                pltpu.SemaphoreType.DMA((2, half)),
                pltpu.SemaphoreType.DMA,
                pltpu.SemaphoreType.DMA,
            ],
            compiler_params=pltpu.CompilerParams(collective_id=0, has_side_effects=True),
        )(
            diffusivity,
            density,
            positions.reshape(1, remnants),
            spectrum.T,
            cell_class.reshape(cells, grid_z),
            operators,
        )
        return out.reshape(bins_all, planes, rows_y // ba_count, grid_z)

    in_specs = (P("ba", "gx", None, None), P("ba"), P(), P(None, "ba"), P("gx", "ba", None), P())
    return jax.shard_map(
        step, mesh=mesh, in_specs=in_specs, out_specs=P(None, "gx", "ba", None), check_vma=False
    )
```

```python
import functools

import jax
import jax.numpy as jnp
from jax import lax
from jax.experimental import pallas as pl
from jax.experimental.pallas import tpu as pltpu
from jax.sharding import PartitionSpec as P

MESH = pl.DeviceIdType.MESH

LOW = 0.1
STEPS = 32767.0
BIAS = 32768

DEPTH = 2


def encode(rho):
    return ((rho - LOW) * STEPS + 0.5).astype(jnp.int32) - BIAS


def decode(code):
    return code.astype(jnp.int32).astype(jnp.float32) * (1.0 / STEPS) + (LOW + BIAS / STEPS)


def yz_sum(field):
    return (
        pltpu.roll(field, 1, 0)
        + pltpu.roll(field, field.shape[0] - 1, 0)
        + pltpu.roll(field, 1, 1)
        + pltpu.roll(field, field.shape[1] - 1, 1)
    )


def kernel(
    gx_count,
    ba_count,
    diff_hbm,
    density_ref,
    pos_hbm,
    spec_hbm,
    class_hbm,
    oper_ref,
    out_ref,
    diff_ref,
    pos_ref,
    spec_ref,
    class_ref,
    dens,
    stage,
    held,
    halo,
    parm_out,
    parm,
    source,
    rounded,
    gathered,
    wide,
    opers,
    weights,
    load_sem,
    swap_send,
    swap_recv,
    parm_send,
    parm_recv,
    halo_send,
    halo_recv,
    spread_send,
    spread_recv,
):
    bins_dev, planes, rows_y, grid_z = density_ref.shape
    half = bins_dev // 2
    ring = 2 * ba_count
    rows_dev = rows_y // ba_count
    bins_all = gathered.shape[0]
    remnants = pos_ref.shape[1]
    part = remnants // 2
    gx = lax.axis_index("gx")
    ba = lax.axis_index("ba")
    side = lax.rem(gx, 2)
    column = gx - side
    me = side * ba_count + ba
    meet = lax.rem(ba + ba_count // 2, ba_count)
    right = lax.rem(gx + 2, gx_count)
    left = lax.rem(gx + gx_count - 2, gx_count)

    barrier = pltpu.get_barrier_semaphore()
    greetings = 0
    for chips in (0, 1, 2, ring // 2 - 2, ring // 2 - 1):
        for core in range(2):
            if chips or core:
                peer = 2 * lax.rem(me // 2 + chips, ring // 2) + lax.rem(me + core, 2)
                pl.semaphore_signal(
                    barrier,
                    inc=1,
                    device_id=(column + peer // ba_count, lax.rem(peer, ba_count)),
                    device_id_type=MESH,
                )
                greetings += 1
    for other in (left, right):
        pl.semaphore_signal(barrier, inc=1, device_id=(other, ba), device_id_type=MESH)
        greetings += 1

    loads = [
        pltpu.make_async_copy(diff_hbm, diff_ref, load_sem.at[0]),
        pltpu.make_async_copy(spec_hbm, spec_ref, load_sem.at[1]),
        pltpu.make_async_copy(
            density_ref.at[pl.ds(0, half)], dens.at[pl.ds(0, half)], load_sem.at[2]
        ),
        pltpu.make_async_copy(
            density_ref.at[pl.ds(half, half)], dens.at[pl.ds(half, half)], load_sem.at[3]
        ),
        pltpu.make_async_copy(pos_hbm, pos_ref, load_sem.at[4]),
        pltpu.make_async_copy(oper_ref, opers, load_sem.at[5]),
        pltpu.make_async_copy(class_hbm, class_ref, load_sem.at[6]),
    ]
    for copy in loads:
        copy.start()

    loads[0].wait()
    loads[1].wait()
    bin_row = lax.broadcasted_iota(jnp.int32, (half, grid_z), 0)
    for h in range(2):
        parm_out[h, :, 0:part] = spec_ref[
            h * half : (h + 1) * half, pl.ds(pl.multiple_of(side * part, part), part)
        ]
        value = jnp.zeros((half, grid_z), jnp.float32)
        for b in range(half):
            value = jnp.where(bin_row == b, diff_ref[h * half + b], value)
        parm_out[h, :, part:] = value
    for h in range(2):
        loads[2 + h].wait()
        for b in range(half):
            stage[h, b] = encode(dens[h * half + b]).astype(jnp.int16)

    pl.semaphore_wait(barrier, greetings)

    swaps = []
    parms = []
    for h in range(2):
        target = (column + h, meet)
        parms.append(
            pltpu.make_async_remote_copy(
                src_ref=parm_out.at[h],
                dst_ref=parm.at[side],
                send_sem=parm_send.at[h],
                recv_sem=parm_recv.at[side],
                device_id=target,
                device_id_type=MESH,
            )
        )
        parms[h].start()
    def swap(b):
        for h in range(2):
            swaps.append(
                pltpu.make_async_remote_copy(
                    src_ref=stage.at[h, b],
                    dst_ref=held.at[side, b],
                    send_sem=swap_send.at[h, b],
                    recv_sem=swap_recv.at[side, b],
                    device_id=(column + h, meet),
                    device_id_type=MESH,
                )
            )
            swaps[-1].start()

    def pump():
        b = len(swaps) // 2
        if b < half:
            for h in range(2):
                swaps[2 * (b - DEPTH) + h].wait_send()
            swap(b)

    for b in range(DEPTH):
        swap(b)

    loads[4].wait()
    loads[5].wait()
    loads[6].wait()
    groups = weights.shape[0] // bins_all
    per_group = weights.shape[1] // bins_all

    def arrange(a, carry):
        weights[pl.ds(pl.multiple_of(a * bins_all, bins_all), bins_all), :] = jnp.concatenate(
            [opers[a * per_group + j] for j in range(per_group)], axis=1
        )
        return carry

    lax.fori_loop(0, groups, arrange, 0)
    pump()

    def wait_parm(s):
        pltpu.make_async_copy(parm.at[s], parm.at[s], parm_recv.at[s]).wait()

    wait_parm(0)
    wait_parm(1)
    planes_col = 2 * planes
    planes_src = planes_col + 2
    pos = pos_ref[...]
    pos_x = pos // (rows_y * grid_z)
    pos_y = lax.rem(pos // grid_z, rows_y)
    pos_z = lax.rem(pos, grid_z)
    width = gx_count * planes
    pos_x = lax.rem(pos_x + (width + 1) - column * planes, width)
    pos_row = pos_x * rows_y + pos_y
    is_row = lax.broadcasted_iota(jnp.int32, (planes_src * rows_y, remnants), 0) == pos_row
    is_z = lax.broadcasted_iota(jnp.int32, (grid_z, remnants), 0) == pos_z
    is_z = jnp.where(is_z, 1.0, 0.0).astype(jnp.bfloat16)
    for b in range(half):
        spec = jnp.concatenate([parm[0, b : b + 1, 0:part], parm[1, b : b + 1, 0:part]], axis=1)
        high = spec.astype(jnp.bfloat16).astype(jnp.float32)
        low = spec - high
        total = jnp.zeros((planes_src * rows_y, grid_z), jnp.float32)
        for piece in (high, low):
            total += lax.dot_general(
                jnp.where(is_row, piece, 0.0).astype(jnp.bfloat16),
                is_z,
                (((1,), (1,)), ((), ())),
                preferred_element_type=jnp.float32,
            )
        source[b] = total.reshape(planes_src, rows_y, grid_z)
        pump()

    halos = [[None, None] for _ in range(half)]

    def forward(b):
        for s in range(2):
            pltpu.make_async_copy(held.at[s, b], held.at[s, b], swap_recv.at[s, b]).wait()
            halos[b][s] = pltpu.make_async_remote_copy(
                src_ref=held.at[s, b],
                dst_ref=halo.at[s, b],
                send_sem=halo_send.at[s, b],
                recv_sem=halo_recv.at[s, b],
                device_id=(left if s == 0 else right, ba),
                device_id_type=MESH,
            )
            halos[b][s].start()

    def diffuse(b):
        for s in range(2):
            halos[b][s].wait_recv()
        rate = parm[0, b : b + 1, part:]
        centre = 1.0 - 6.0 * rate
        fields = [decode(halo[1, b, p]) for p in range(planes)]
        fields += [decode(held[s, b, p]) for s in range(2) for p in range(planes)]
        fields += [decode(halo[0, b, p]) for p in range(planes)]
        sources = [source[b, p] for p in range(planes_src)]
        first = [
            centre * fields[p + 1] + rate * (fields[p] + fields[p + 2] + yz_sum(fields[p + 1])) + sources[p]
            for p in range(planes_src)
        ]
        second = [
            centre * first[p + 1]
            + rate * (first[p] + first[p + 2] + yz_sum(first[p + 1]))
            + sources[p + 1]
            for p in range(planes_col)
        ]
        for s in range(2):
            block = jnp.concatenate(
                [second[s * planes + p].reshape(ba_count, rows_dev, grid_z) for p in range(planes)],
                axis=1,
            )
            rounded[b, pl.ds(s * ba_count, ba_count)] = block.astype(jnp.bfloat16)

    group = 2 * meet + side

    def spread(b):
        slot = gathered.at[group * half + b]
        for offset in list(range(ring // 2, ring)) + list(range(1, ring // 2)):
            peer = lax.rem(me + offset, ring)
            pltpu.make_async_remote_copy(
                src_ref=rounded.at[b, peer],
                dst_ref=slot,
                send_sem=spread_send,
                recv_sem=spread_recv,
                device_id=(column + peer // ba_count, lax.rem(peer, ba_count)),
                device_id_type=MESH,
            ).start()
        pltpu.make_async_copy(rounded.at[b, me], slot, spread_recv).start()

    forward(0)
    for b in range(half):
        if b + 1 < half:
            forward(b + 1)
        diffuse(b)
        spread(b)

    pltpu.make_async_copy(gathered, gathered, spread_recv).wait()

    wide[...] = gathered[...].astype(jnp.float32).reshape(wide.shape)
    cells = planes * rows_dev

    def update(step, carry):
        first_row = 2 * step
        values = jnp.concatenate(
            [wide[pl.ds(first_row + j, bins_all, stride=cells), :] for j in range(2)], axis=1
        )
        classes = jnp.concatenate([class_ref[pl.ds(first_row + j, 1), :] for j in range(2)], axis=1)
        within = lax.rem(classes, per_group)
        outer = classes // per_group
        stacked = jnp.concatenate(
            [jnp.where(within == j, values, 0.0) for j in range(per_group)], axis=0
        ).astype(jnp.bfloat16)
        products = jnp.dot(weights[...], stacked, preferred_element_type=jnp.float32)
        result = products[0:bins_all]
        for a in range(1, groups):
            result = jnp.where(outer == a, products[a * bins_all : (a + 1) * bins_all], result)
        for j in range(2):
            out_ref[pl.ds(first_row + j, bins_all, stride=cells), :] = result[
                :, j * grid_z : (j + 1) * grid_z
            ]
        return carry

    lax.fori_loop(0, cells // 2, update, 0)

    for copy in parms + swaps[2 * (half - DEPTH) :]:
        copy.wait_send()
    for b in range(half):
        for s in range(2):
            halos[b][s].wait_send()
    sent = rounded.at[:, pl.ds(0, ring - 1)]
    pltpu.make_async_copy(sent, sent, spread_send).wait()


def solution(mesh):
    gx_count, ba_count = mesh.shape["gx"], mesh.shape["ba"]

    def step(density, diffusivity, positions, spectrum, cell_class, operators):
        bins_dev, planes, rows_y, grid_z = density.shape
        classes, bins_all, _ = operators.shape
        remnants = positions.shape[0]
        half = bins_dev // 2
        cells = planes * (rows_y // ba_count)
        per_group = 4
        vmem = pl.BlockSpec(memory_space=pltpu.VMEM)
        out = pl.pallas_call(
            functools.partial(kernel, gx_count, ba_count),
            out_shape=jax.ShapeDtypeStruct((bins_all * cells, grid_z), jnp.float32),
            in_specs=[pl.BlockSpec(memory_space=pltpu.HBM)] * 6,
            out_specs=vmem,
            scratch_shapes=[
                pltpu.SMEM((bins_dev,), jnp.float32),
                pltpu.VMEM((1, remnants), jnp.int32),
                pltpu.VMEM((bins_dev, remnants), jnp.float32),
                pltpu.VMEM((cells, grid_z), jnp.int32),
                pltpu.VMEM(density.shape, jnp.float32),
                pltpu.VMEM((2, half, planes, rows_y, grid_z), jnp.int16),
                pltpu.VMEM((2, half, planes, rows_y, grid_z), jnp.int16),
                pltpu.VMEM((2, half, planes, rows_y, grid_z), jnp.int16),
                pltpu.VMEM((2, half, remnants // 2 + grid_z), jnp.float32),
                pltpu.VMEM((2, half, remnants // 2 + grid_z), jnp.float32),
                pltpu.VMEM((half, 2 * planes + 2, rows_y, grid_z), jnp.float32),
                pltpu.VMEM((half, 2 * ba_count, cells, grid_z), jnp.bfloat16),
                pltpu.VMEM((bins_all, cells, grid_z), jnp.bfloat16),
                pltpu.VMEM((bins_all * cells, grid_z), jnp.float32),
                pltpu.VMEM(operators.shape, jnp.bfloat16),
                pltpu.VMEM((classes // per_group * bins_all, per_group * bins_all), jnp.bfloat16),
                pltpu.SemaphoreType.DMA((7,)),
                pltpu.SemaphoreType.DMA((2, half)),
                pltpu.SemaphoreType.DMA((2, half)),
                pltpu.SemaphoreType.DMA((2,)),
                pltpu.SemaphoreType.DMA((2,)),
                pltpu.SemaphoreType.DMA((2, half)),
                pltpu.SemaphoreType.DMA((2, half)),
                pltpu.SemaphoreType.DMA,
                pltpu.SemaphoreType.DMA,
            ],
            compiler_params=pltpu.CompilerParams(
                collective_id=0, has_side_effects=True, vmem_limit_bytes=16 * 2**20
            ),
        )(
            *[
                pltpu.with_memory_space_constraint(operand, pltpu.HBM)
                for operand in (
                    diffusivity,
                    density,
                    positions.reshape(1, remnants),
                    spectrum.T,
                    cell_class.reshape(cells, grid_z),
                    operators,
                )
            ]
        )
        return out.reshape(bins_all, planes, rows_y // ba_count, grid_z)

    in_specs = (P("ba", "gx", None, None), P("ba"), P(), P(None, "ba"), P("gx", "ba", None), P())
    return jax.shard_map(
        step, mesh=mesh, in_specs=in_specs, out_specs=P(None, "gx", "ba", None), check_vma=False
    )
```

```python
import functools

import jax
import jax.numpy as jnp
from jax import lax
from jax.experimental import pallas as pl
from jax.experimental.pallas import tpu as pltpu
from jax.sharding import PartitionSpec as P

MESH = pl.DeviceIdType.MESH

LOW = 0.1
STEPS = 32767.0
BIAS = 32768


def encode(rho):
    return ((rho - LOW) * STEPS + 0.5).astype(jnp.int32) - BIAS


def decode(code):
    return code.astype(jnp.int32).astype(jnp.float32) * (1.0 / STEPS) + (LOW + BIAS / STEPS)


def yz_sum(field):
    return (
        pltpu.roll(field, 1, 0)
        + pltpu.roll(field, field.shape[0] - 1, 0)
        + pltpu.roll(field, 1, 1)
        + pltpu.roll(field, field.shape[1] - 1, 1)
    )


def kernel(
    gx_count,
    ba_count,
    diff_hbm,
    density_ref,
    pos_hbm,
    spec_hbm,
    class_hbm,
    oper_ref,
    out_ref,
    diff_ref,
    pos_ref,
    spec_ref,
    class_ref,
    dens,
    stage,
    held,
    halo,
    parm_out,
    parm,
    source,
    rounded,
    gathered,
    wide,
    sums,
    opers,
    weights,
    chunk_weights,
    load_sem,
    swap_send,
    swap_recv,
    parm_send,
    parm_recv,
    halo_send,
    halo_recv,
    spread_send,
    spread_recv,
):
    bins_dev, planes, rows_y, grid_z = density_ref.shape
    half = bins_dev // 2
    ring = 2 * ba_count
    rows_dev = rows_y // ba_count
    bins_all = opers.shape[1]
    remnants = pos_ref.shape[1]
    part = remnants // 2
    gx = lax.axis_index("gx")
    ba = lax.axis_index("ba")
    side = lax.rem(gx, 2)
    column = gx - side
    me = side * ba_count + ba
    meet = lax.rem(ba + ba_count // 2, ba_count)
    right = lax.rem(gx + 2, gx_count)
    left = lax.rem(gx + gx_count - 2, gx_count)

    barrier = pltpu.get_barrier_semaphore()
    greetings = 0
    for chips in (0, 1, 2, ring // 2 - 2, ring // 2 - 1):
        for core in range(2):
            if chips or core:
                peer = 2 * lax.rem(me // 2 + chips, ring // 2) + lax.rem(me + core, 2)
                pl.semaphore_signal(
                    barrier,
                    inc=1,
                    device_id=(column + peer // ba_count, lax.rem(peer, ba_count)),
                    device_id_type=MESH,
                )
                greetings += 1
    for other in (left, right):
        pl.semaphore_signal(barrier, inc=1, device_id=(other, ba), device_id_type=MESH)
        greetings += 1

    loads = [
        pltpu.make_async_copy(diff_hbm, diff_ref, load_sem.at[0]),
        pltpu.make_async_copy(spec_hbm, spec_ref, load_sem.at[1]),
        pltpu.make_async_copy(pos_hbm, pos_ref, load_sem.at[2]),
        pltpu.make_async_copy(oper_ref, opers, load_sem.at[3]),
        pltpu.make_async_copy(class_hbm, class_ref, load_sem.at[4]),
    ]
    loads += [
        pltpu.make_async_copy(
            density_ref.at[h * half + b], dens.at[h * half + b], load_sem.at[5 + h * half + b]
        )
        for b in range(half)
        for h in range(2)
    ]
    for copy in loads[:2] + loads[5:] + loads[2:5]:
        copy.start()

    loads[0].wait()
    loads[1].wait()
    bin_row = lax.broadcasted_iota(jnp.int32, (half, grid_z), 0)
    for h in range(2):
        parm_out[h, :, 0:part] = spec_ref[
            h * half : (h + 1) * half, pl.ds(pl.multiple_of(side * part, part), part)
        ]
        value = jnp.zeros((half, grid_z), jnp.float32)
        for b in range(half):
            value = jnp.where(bin_row == b, diff_ref[h * half + b], value)
        parm_out[h, :, part:] = value
    swaps = []

    def encode_chunk(b):
        for h in range(2):
            loads[5 + 2 * b + h].wait()
            stage[h, b] = encode(dens[h * half + b]).astype(jnp.int16)

    def swap(b):
        for h in range(2):
            swaps.append(
                pltpu.make_async_remote_copy(
                    src_ref=stage.at[h, b],
                    dst_ref=held.at[side, b],
                    send_sem=swap_send.at[h, b],
                    recv_sem=swap_recv.at[side, b],
                    device_id=(column + h, meet),
                    device_id_type=MESH,
                )
            )
            swaps[-1].start()

    encode_chunk(0)
    pl.semaphore_wait(barrier, greetings)

    parms = []
    for h in range(2):
        target = (column + h, meet)
        parms.append(
            pltpu.make_async_remote_copy(
                src_ref=parm_out.at[h],
                dst_ref=parm.at[side],
                send_sem=parm_send.at[h],
                recv_sem=parm_recv.at[side],
                device_id=target,
                device_id_type=MESH,
            )
        )
        parms[h].start()
    swap(0)
    for b in range(1, half):
        encode_chunk(b)

    loads[2].wait()
    loads[3].wait()
    loads[4].wait()
    quad = weights.shape[1] // bins_all
    quads = weights.shape[0] // bins_all

    def arrange(a, carry):
        weights[pl.ds(pl.multiple_of(a * bins_all, bins_all), bins_all), :] = jnp.concatenate(
            [opers[a * quad + j] for j in range(quad)], axis=1
        )
        return carry

    lax.fori_loop(0, quads // 2, arrange, 0)
    swap(1)
    lax.fori_loop(quads // 2, quads, arrange, 0)

    planes_col = 2 * planes
    planes_src = planes_col + 2
    pos = pos_ref[...]
    pos_x = pos // (rows_y * grid_z)
    pos_y = lax.rem(pos // grid_z, rows_y)
    pos_z = lax.rem(pos, grid_z)
    width = gx_count * planes
    pos_x = lax.rem(pos_x + (width + 1) - column * planes, width)
    pos_row = pos_x * rows_y + pos_y
    is_row = lax.broadcasted_iota(jnp.int32, (planes_src * rows_y, remnants), 0) == pos_row
    is_row = jnp.where(is_row, 1.0, 0.0).astype(jnp.bfloat16)
    is_z = lax.broadcasted_iota(jnp.int32, (grid_z, remnants), 0) == pos_z
    swap(2)
    for s in range(2):
        pltpu.make_async_copy(parm.at[s], parm.at[s], parm_recv.at[s]).wait()
    swap(3)
    spec = jnp.concatenate([parm[0, :, 0:part], parm[1, :, 0:part]], axis=1)
    high = spec.astype(jnp.bfloat16).astype(jnp.float32)
    low = spec - high

    def inject(pair):
        total = jnp.zeros((planes_src * rows_y, 2 * grid_z), jnp.float32)
        for piece in (high, low):
            placed = [
                jnp.where(is_z, piece[b : b + 1], 0.0).astype(jnp.bfloat16)
                for b in (2 * pair, 2 * pair + 1)
            ]
            total += lax.dot_general(
                is_row,
                jnp.concatenate(placed, axis=0),
                (((1,), (1,)), ((), ())),
                preferred_element_type=jnp.float32,
            )
        for j in range(2):
            source[2 * pair + j] = total[:, j * grid_z : (j + 1) * grid_z].reshape(
                planes_src, rows_y, grid_z
            )

    halos = [[None, None] for _ in range(half)]

    def forward(b):
        for s in range(2):
            pltpu.make_async_copy(held.at[s, b], held.at[s, b], swap_recv.at[s, b]).wait()
            halos[b][s] = pltpu.make_async_remote_copy(
                src_ref=held.at[s, b],
                dst_ref=halo.at[s, b],
                send_sem=halo_send.at[s, b],
                recv_sem=halo_recv.at[s, b],
                device_id=(left if s == 0 else right, ba),
                device_id_type=MESH,
            )
            halos[b][s].start()

    low_classes = chunk_weights.shape[2] // ring
    high_classes = chunk_weights.shape[1] // bins_all

    def regroup():
        size = weights.shape[1]
        k = lax.broadcasted_iota(jnp.int32, (size, size), 0)
        n = lax.broadcasted_iota(jnp.int32, (size, size), 1)
        wanted = (n // bins_all) + half * lax.rem(n, ring)
        pick = (k // bins_all == lax.rem(n, bins_all) // ring) & (lax.rem(k, bins_all) == wanted)
        pick = jnp.where(pick, 1.0, 0.0).astype(jnp.bfloat16)
        per_high = low_classes // quad

        def one(a, carry):
            rows = pl.ds(pl.multiple_of(a * per_high * bins_all, bins_all), per_high * bins_all)
            picked = jnp.dot(weights[rows, :], pick, preferred_element_type=jnp.float32)
            picked = picked.astype(jnp.bfloat16)
            place = pl.ds(pl.multiple_of(a * bins_all, bins_all), bins_all)
            for b in range(half):
                chunk_weights[b, place, :] = jnp.concatenate(
                    [
                        picked[t * bins_all : (t + 1) * bins_all, b * bins_all : (b + 1) * bins_all]
                        for t in range(per_high)
                    ],
                    axis=1,
                )
            return carry

        lax.fori_loop(0, high_classes, one, 0)

    def diffuse(b):
        for s in range(2):
            halos[b][s].wait_recv()
        rate = parm[0, b : b + 1, part:]
        centre = 1.0 - 6.0 * rate
        fields = [decode(halo[1, b, p]) for p in range(planes)]
        fields += [decode(held[s, b, p]) for s in range(2) for p in range(planes)]
        fields += [decode(halo[0, b, p]) for p in range(planes)]
        sources = [source[b, p] for p in range(planes_src)]
        first = [
            centre * fields[p + 1] + rate * (fields[p] + fields[p + 2] + yz_sum(fields[p + 1])) + sources[p]
            for p in range(planes_src)
        ]
        second = [
            centre * first[p + 1]
            + rate * (first[p] + first[p + 2] + yz_sum(first[p + 1]))
            + sources[p + 1]
            for p in range(planes_col)
        ]
        for s in range(2):
            block = jnp.concatenate(
                [second[s * planes + p].reshape(ba_count, rows_dev, grid_z) for p in range(planes)],
                axis=1,
            )
            rounded[b, pl.ds(s * ba_count, ba_count)] = block.astype(jnp.bfloat16)

    group = 2 * meet + side

    def spread(b):
        slot = gathered.at[b, group]
        for offset in list(range(ring // 2, ring)) + list(range(1, ring // 2)):
            peer = lax.rem(me + offset, ring)
            pltpu.make_async_remote_copy(
                src_ref=rounded.at[b, peer],
                dst_ref=slot,
                send_sem=spread_send,
                recv_sem=spread_recv.at[b],
                device_id=(column + peer // ba_count, lax.rem(peer, ba_count)),
                device_id_type=MESH,
            ).start()
        pltpu.make_async_copy(rounded.at[b, me], slot, spread_recv.at[b]).start()

    forward(0)
    inject(0)
    forward(1)
    inject(1)
    forward(2)
    regroup()
    diffuse(0)
    spread(0)
    forward(3)
    for b in range(1, half):
        diffuse(b)
        spread(b)

    cells = planes * rows_dev

    def update(b):
        pltpu.make_async_copy(gathered.at[b], gathered.at[b], spread_recv.at[b]).wait()
        wide[...] = gathered[b].astype(jnp.float32).reshape(wide.shape)

        def pair(step, carry):
            first_row = 2 * step
            values = jnp.concatenate(
                [wide[pl.ds(first_row + j, ring, stride=cells), :] for j in range(2)], axis=1
            )
            classes = jnp.concatenate(
                [class_ref[pl.ds(first_row + j, 1), :] for j in range(2)], axis=1
            )
            low_class = lax.rem(classes, low_classes)
            high_class = classes // low_classes
            stacked = jnp.concatenate(
                [jnp.where(low_class == j, values, 0.0) for j in range(low_classes)], axis=0
            ).astype(jnp.bfloat16)
            products = jnp.dot(chunk_weights[b], stacked, preferred_element_type=jnp.float32)
            result = products[0:bins_all]
            for a in range(1, high_classes):
                result = jnp.where(
                    high_class == a, products[a * bins_all : (a + 1) * bins_all], result
                )
            if b > 0:
                result += sums[step]
            if b < half - 1:
                sums[step] = result
            else:
                for j in range(2):
                    out_ref[pl.ds(first_row + j, bins_all, stride=cells), :] = result[
                        :, j * grid_z : (j + 1) * grid_z
                    ]
            return carry

        lax.fori_loop(0, cells // 2, pair, 0, unroll=8)

    for b in range(half):
        update(b)

    for copy in parms + swaps:
        copy.wait_send()
    for b in range(half):
        for s in range(2):
            halos[b][s].wait_send()
    sent = rounded.at[:, pl.ds(0, ring - 1)]
    pltpu.make_async_copy(sent, sent, spread_send).wait()


def solution(mesh):
    gx_count, ba_count = mesh.shape["gx"], mesh.shape["ba"]

    def step(density, diffusivity, positions, spectrum, cell_class, operators):
        bins_dev, planes, rows_y, grid_z = density.shape
        classes, bins_all, _ = operators.shape
        remnants = positions.shape[0]
        half = bins_dev // 2
        cells = planes * (rows_y // ba_count)
        quad, low_classes = 4, 16
        vmem = pl.BlockSpec(memory_space=pltpu.VMEM)
        out = pl.pallas_call(
            functools.partial(kernel, gx_count, ba_count),
            out_shape=jax.ShapeDtypeStruct((bins_all * cells, grid_z), jnp.float32),
            in_specs=[pl.BlockSpec(memory_space=pltpu.HBM)] * 6,
            out_specs=vmem,
            scratch_shapes=[
                pltpu.SMEM((bins_dev,), jnp.float32),
                pltpu.VMEM((1, remnants), jnp.int32),
                pltpu.VMEM((bins_dev, remnants), jnp.float32),
                pltpu.VMEM((cells, grid_z), jnp.int32),
                pltpu.VMEM(density.shape, jnp.float32),
                pltpu.VMEM((2, half, planes, rows_y, grid_z), jnp.int16),
                pltpu.VMEM((2, half, planes, rows_y, grid_z), jnp.int16),
                pltpu.VMEM((2, half, planes, rows_y, grid_z), jnp.int16),
                pltpu.VMEM((2, half, remnants // 2 + grid_z), jnp.float32),
                pltpu.VMEM((2, half, remnants // 2 + grid_z), jnp.float32),
                pltpu.VMEM((half, 2 * planes + 2, rows_y, grid_z), jnp.float32),
                pltpu.VMEM((half, 2 * ba_count, cells, grid_z), jnp.bfloat16),
                pltpu.VMEM((half, 2 * ba_count, cells, grid_z), jnp.bfloat16),
                pltpu.VMEM((2 * ba_count * cells, grid_z), jnp.float32),
                pltpu.VMEM((cells // 2, bins_all, 2 * grid_z), jnp.float32),
                pltpu.VMEM(operators.shape, jnp.bfloat16),
                pltpu.VMEM((classes // quad * bins_all, quad * bins_all), jnp.bfloat16),
                pltpu.VMEM((half, classes // low_classes * bins_all, low_classes * 2 * ba_count), jnp.bfloat16),
                pltpu.SemaphoreType.DMA((5 + bins_dev,)),
                pltpu.SemaphoreType.DMA((2, half)),
                pltpu.SemaphoreType.DMA((2, half)),
                pltpu.SemaphoreType.DMA((2,)),
                pltpu.SemaphoreType.DMA((2,)),
                pltpu.SemaphoreType.DMA((2, half)),
                pltpu.SemaphoreType.DMA((2, half)),
                pltpu.SemaphoreType.DMA,
                pltpu.SemaphoreType.DMA((half,)),
            ],
            compiler_params=pltpu.CompilerParams(
                collective_id=0, has_side_effects=True, vmem_limit_bytes=16 * 2**20
            ),
        )(
            *[
                pltpu.with_memory_space_constraint(operand, pltpu.HBM)
                for operand in (
                    diffusivity,
                    density,
                    positions.reshape(1, remnants),
                    spectrum.T,
                    cell_class.reshape(cells, grid_z),
                    operators,
                )
            ]
        )
        return out.reshape(bins_all, planes, rows_y // ba_count, grid_z)

    in_specs = (P("ba", "gx", None, None), P("ba"), P(), P(None, "ba"), P("gx", "ba", None), P())
    return jax.shard_map(
        step, mesh=mesh, in_specs=in_specs, out_specs=P(None, "gx", "ba", None), check_vma=False
    )
```

```python
import functools

import jax
import jax.numpy as jnp
from jax import lax
from jax.experimental import pallas as pl
from jax.experimental.pallas import tpu as pltpu
from jax.sharding import PartitionSpec as P

MESH = pl.DeviceIdType.MESH

LOW = 0.1
STEPS = 32767.0
BIAS = 32768


def encode(rho):
    return ((rho - LOW) * STEPS + 0.5).astype(jnp.int32) - BIAS


def decode(code):
    return code.astype(jnp.int32).astype(jnp.float32) * (1.0 / STEPS) + (LOW + BIAS / STEPS)


def yz_sum(field):
    return (
        pltpu.roll(field, 1, 0)
        + pltpu.roll(field, field.shape[0] - 1, 0)
        + pltpu.roll(field, 1, 1)
        + pltpu.roll(field, field.shape[1] - 1, 1)
    )


def kernel(
    gx_count,
    ba_count,
    diff_hbm,
    density_ref,
    pos_hbm,
    spec_hbm,
    class_hbm,
    oper_ref,
    out_ref,
    diff_ref,
    pos_ref,
    spec_ref,
    class_ref,
    dens,
    stage,
    held,
    halo,
    parm_out,
    parm,
    source,
    rounded,
    gathered,
    wide,
    sums,
    opers,
    weights,
    chunk_weights,
    load_sem,
    swap_send,
    swap_recv,
    parm_send,
    parm_recv,
    halo_send,
    halo_recv,
    spread_send,
    spread_recv,
):
    bins_dev, planes, rows_y, grid_z = density_ref.shape
    half = bins_dev // 2
    ring = 2 * ba_count
    rows_dev = rows_y // ba_count
    bins_all = opers.shape[1]
    remnants = pos_ref.shape[1]
    part = remnants // 2
    gx = lax.axis_index("gx")
    ba = lax.axis_index("ba")
    side = lax.rem(gx, 2)
    column = gx - side
    me = side * ba_count + ba
    meet = lax.rem(ba + ba_count // 2, ba_count)
    right = lax.rem(gx + 2, gx_count)
    left = lax.rem(gx + gx_count - 2, gx_count)

    barrier = pltpu.get_barrier_semaphore()
    greetings = 0
    for chips in (0, 1, 2, ring // 2 - 2, ring // 2 - 1):
        for core in range(2):
            if chips or core:
                peer = 2 * lax.rem(me // 2 + chips, ring // 2) + lax.rem(me + core, 2)
                pl.semaphore_signal(
                    barrier,
                    inc=1,
                    device_id=(column + peer // ba_count, lax.rem(peer, ba_count)),
                    device_id_type=MESH,
                )
                greetings += 1
    for other in (left, right):
        pl.semaphore_signal(barrier, inc=1, device_id=(other, ba), device_id_type=MESH)
        greetings += 1

    loads = [
        pltpu.make_async_copy(diff_hbm, diff_ref, load_sem.at[0]),
        pltpu.make_async_copy(spec_hbm, spec_ref, load_sem.at[1]),
        pltpu.make_async_copy(pos_hbm, pos_ref, load_sem.at[2]),
        pltpu.make_async_copy(oper_ref, opers, load_sem.at[3]),
        pltpu.make_async_copy(class_hbm, class_ref, load_sem.at[4]),
    ]
    loads += [
        pltpu.make_async_copy(
            density_ref.at[h * half + b], dens.at[h * half + b], load_sem.at[5 + h * half + b]
        )
        for b in range(half)
        for h in range(2)
    ]
    for copy in loads[:2] + loads[5:] + loads[2:5]:
        copy.start()

    loads[0].wait()
    loads[1].wait()
    bin_row = lax.broadcasted_iota(jnp.int32, (half, grid_z), 0)
    for h in range(2):
        parm_out[h, :, 0:part] = spec_ref[
            h * half : (h + 1) * half, pl.ds(pl.multiple_of(side * part, part), part)
        ]
        value = jnp.zeros((half, grid_z), jnp.float32)
        for b in range(half):
            value = jnp.where(bin_row == b, diff_ref[h * half + b], value)
        parm_out[h, :, part:] = value
    swaps = []

    def encode_chunk(b):
        for h in range(2):
            loads[5 + 2 * b + h].wait()
            stage[h, b] = encode(dens[h * half + b]).astype(jnp.int16)

    def swap(b):
        for h in range(2):
            swaps.append(
                pltpu.make_async_remote_copy(
                    src_ref=stage.at[h, b],
                    dst_ref=held.at[side, b],
                    send_sem=swap_send.at[h, b],
                    recv_sem=swap_recv.at[side, b],
                    device_id=(column + h, meet),
                    device_id_type=MESH,
                )
            )
            swaps[-1].start()

    encode_chunk(0)
    pl.semaphore_wait(barrier, greetings)

    parms = []
    for h in range(2):
        target = (column + h, meet)
        parms.append(
            pltpu.make_async_remote_copy(
                src_ref=parm_out.at[h],
                dst_ref=parm.at[side],
                send_sem=parm_send.at[h],
                recv_sem=parm_recv.at[side],
                device_id=target,
                device_id_type=MESH,
            )
        )
        parms[h].start()
    swap(0)
    for b in range(1, half):
        encode_chunk(b)

    loads[2].wait()
    loads[3].wait()
    loads[4].wait()
    quad = weights.shape[1] // bins_all
    quads = weights.shape[0] // bins_all

    def arrange(a, carry):
        weights[pl.ds(pl.multiple_of(a * bins_all, bins_all), bins_all), :] = jnp.concatenate(
            [opers[a * quad + j] for j in range(quad)], axis=1
        )
        return carry

    lax.fori_loop(0, quads // 2, arrange, 0)
    swap(1)
    lax.fori_loop(quads // 2, quads, arrange, 0)

    planes_col = 2 * planes
    planes_src = planes_col + 2
    pos = pos_ref[...]
    pos_x = pos // (rows_y * grid_z)
    pos_y = lax.rem(pos // grid_z, rows_y)
    pos_z = lax.rem(pos, grid_z)
    width = gx_count * planes
    pos_x = lax.rem(pos_x + (width + 1) - column * planes, width)
    pos_row = pos_x * rows_y + pos_y
    is_row = lax.broadcasted_iota(jnp.int32, (planes_src * rows_y, remnants), 0) == pos_row
    is_row = jnp.where(is_row, 1.0, 0.0).astype(jnp.bfloat16)
    is_z = lax.broadcasted_iota(jnp.int32, (grid_z, remnants), 0) == pos_z
    swap(2)
    for s in range(2):
        pltpu.make_async_copy(parm.at[s], parm.at[s], parm_recv.at[s]).wait()
    swap(3)
    spec = jnp.concatenate([parm[0, :, 0:part], parm[1, :, 0:part]], axis=1)
    high = spec.astype(jnp.bfloat16).astype(jnp.float32)
    low = spec - high

    def inject(pair):
        total = jnp.zeros((planes_src * rows_y, 2 * grid_z), jnp.float32)
        for piece in (high, low):
            placed = [
                jnp.where(is_z, piece[b : b + 1], 0.0).astype(jnp.bfloat16)
                for b in (2 * pair, 2 * pair + 1)
            ]
            total += lax.dot_general(
                is_row,
                jnp.concatenate(placed, axis=0),
                (((1,), (1,)), ((), ())),
                preferred_element_type=jnp.float32,
            )
        for j in range(2):
            source[2 * pair + j] = total[:, j * grid_z : (j + 1) * grid_z].reshape(
                planes_src, rows_y, grid_z
            )

    halos = [[None, None] for _ in range(half)]

    def forward(b):
        for s in range(2):
            pltpu.make_async_copy(held.at[s, b], held.at[s, b], swap_recv.at[s, b]).wait()
            halos[b][s] = pltpu.make_async_remote_copy(
                src_ref=held.at[s, b],
                dst_ref=halo.at[s, b],
                send_sem=halo_send.at[s, b],
                recv_sem=halo_recv.at[s, b],
                device_id=(left if s == 0 else right, ba),
                device_id_type=MESH,
            )
            halos[b][s].start()

    low_classes = chunk_weights.shape[2] // ring
    high_classes = chunk_weights.shape[1] // bins_all

    def regroup():
        size = weights.shape[1]
        k = lax.broadcasted_iota(jnp.int32, (size, size), 0)
        n = lax.broadcasted_iota(jnp.int32, (size, size), 1)
        wanted = (n // bins_all) + half * lax.rem(n, ring)
        pick = (k // bins_all == lax.rem(n, bins_all) // ring) & (lax.rem(k, bins_all) == wanted)
        pick = jnp.where(pick, 1.0, 0.0).astype(jnp.bfloat16)
        per_high = low_classes // quad

        def one(a, carry):
            rows = pl.ds(pl.multiple_of(a * per_high * bins_all, bins_all), per_high * bins_all)
            picked = jnp.dot(weights[rows, :], pick, preferred_element_type=jnp.float32)
            picked = picked.astype(jnp.bfloat16)
            place = pl.ds(pl.multiple_of(a * bins_all, bins_all), bins_all)
            for b in range(half):
                chunk_weights[b, place, :] = jnp.concatenate(
                    [
                        picked[t * bins_all : (t + 1) * bins_all, b * bins_all : (b + 1) * bins_all]
                        for t in range(per_high)
                    ],
                    axis=1,
                )
            return carry

        lax.fori_loop(0, high_classes, one, 0)

    def diffuse(b):
        for s in range(2):
            halos[b][s].wait_recv()
        rate = parm[0, b : b + 1, part:]
        centre = 1.0 - 6.0 * rate
        fields = [decode(halo[1, b, p]) for p in range(planes)]
        fields += [decode(held[s, b, p]) for s in range(2) for p in range(planes)]
        fields += [decode(halo[0, b, p]) for p in range(planes)]
        sources = [source[b, p] for p in range(planes_src)]
        first = [
            centre * fields[p + 1] + rate * (fields[p] + fields[p + 2] + yz_sum(fields[p + 1])) + sources[p]
            for p in range(planes_src)
        ]
        second = [
            centre * first[p + 1]
            + rate * (first[p] + first[p + 2] + yz_sum(first[p + 1]))
            + sources[p + 1]
            for p in range(planes_col)
        ]
        for s in range(2):
            block = jnp.concatenate(
                [second[s * planes + p].reshape(ba_count, rows_dev, grid_z) for p in range(planes)],
                axis=1,
            )
            rounded[b, pl.ds(s * ba_count, ba_count)] = block.astype(jnp.bfloat16)

    group = 2 * meet + side
    peers = []
    for offset in sorted(range(1, ring), key=lambda o: -min(o, ring - o)):
        peer = lax.rem(me + offset, ring)
        peers.append((peer, (column + peer // ba_count, lax.rem(peer, ba_count))))

    def spread(b):
        slot = gathered.at[b, group]
        for peer, place in peers:
            pltpu.make_async_remote_copy(
                src_ref=rounded.at[b, peer],
                dst_ref=slot,
                send_sem=spread_send,
                recv_sem=spread_recv.at[b],
                device_id=place,
                device_id_type=MESH,
            ).start()
        pltpu.make_async_copy(rounded.at[b, me], slot, spread_recv.at[b]).start()

    forward(0)
    inject(0)
    forward(1)
    inject(1)
    forward(2)
    forward(3)
    diffuse(0)
    spread(0)
    diffuse(1)
    spread(1)
    diffuse(2)
    spread(2)
    diffuse(3)
    spread(3)
    regroup()

    cells = planes * rows_dev

    def update(b):
        pltpu.make_async_copy(gathered.at[b], gathered.at[b], spread_recv.at[b]).wait()
        wide[...] = gathered[b].astype(jnp.float32).reshape(wide.shape)

        def pair(step, carry):
            first_row = 2 * step
            values = jnp.concatenate(
                [wide[pl.ds(first_row + j, ring, stride=cells), :] for j in range(2)], axis=1
            )
            classes = jnp.concatenate(
                [class_ref[pl.ds(first_row + j, 1), :] for j in range(2)], axis=1
            )
            low_class = lax.rem(classes, low_classes)
            high_class = classes // low_classes
            stacked = jnp.concatenate(
                [jnp.where(low_class == j, values, 0.0) for j in range(low_classes)], axis=0
            ).astype(jnp.bfloat16)
            products = jnp.dot(chunk_weights[b], stacked, preferred_element_type=jnp.float32)
            result = products[0:bins_all]
            for a in range(1, high_classes):
                result = jnp.where(
                    high_class == a, products[a * bins_all : (a + 1) * bins_all], result
                )
            if b > 0:
                result += sums[step]
            if b < half - 1:
                sums[step] = result
            else:
                for j in range(2):
                    out_ref[pl.ds(first_row + j, bins_all, stride=cells), :] = result[
                        :, j * grid_z : (j + 1) * grid_z
                    ]
            return carry

        lax.fori_loop(0, cells // 2, pair, 0, unroll=8)

    for b in range(half):
        update(b)

    for copy in parms + swaps:
        copy.wait_send()
    for b in range(half):
        for s in range(2):
            halos[b][s].wait_send()
    sent = rounded.at[:, pl.ds(0, ring - 1)]
    pltpu.make_async_copy(sent, sent, spread_send).wait()


def solution(mesh):
    gx_count, ba_count = mesh.shape["gx"], mesh.shape["ba"]

    def step(density, diffusivity, positions, spectrum, cell_class, operators):
        bins_dev, planes, rows_y, grid_z = density.shape
        classes, bins_all, _ = operators.shape
        remnants = positions.shape[0]
        half = bins_dev // 2
        cells = planes * (rows_y // ba_count)
        quad, low_classes = 4, 16
        vmem = pl.BlockSpec(memory_space=pltpu.VMEM)
        out = pl.pallas_call(
            functools.partial(kernel, gx_count, ba_count),
            out_shape=jax.ShapeDtypeStruct((bins_all * cells, grid_z), jnp.float32),
            in_specs=[pl.BlockSpec(memory_space=pltpu.HBM)] * 6,
            out_specs=vmem,
            scratch_shapes=[
                pltpu.SMEM((bins_dev,), jnp.float32),
                pltpu.VMEM((1, remnants), jnp.int32),
                pltpu.VMEM((bins_dev, remnants), jnp.float32),
                pltpu.VMEM((cells, grid_z), jnp.int32),
                pltpu.VMEM(density.shape, jnp.float32),
                pltpu.VMEM((2, half, planes, rows_y, grid_z), jnp.int16),
                pltpu.VMEM((2, half, planes, rows_y, grid_z), jnp.int16),
                pltpu.VMEM((2, half, planes, rows_y, grid_z), jnp.int16),
                pltpu.VMEM((2, half, remnants // 2 + grid_z), jnp.float32),
                pltpu.VMEM((2, half, remnants // 2 + grid_z), jnp.float32),
                pltpu.VMEM((half, 2 * planes + 2, rows_y, grid_z), jnp.float32),
                pltpu.VMEM((half, 2 * ba_count, cells, grid_z), jnp.bfloat16),
                pltpu.VMEM((half, 2 * ba_count, cells, grid_z), jnp.bfloat16),
                pltpu.VMEM((2 * ba_count * cells, grid_z), jnp.float32),
                pltpu.VMEM((cells // 2, bins_all, 2 * grid_z), jnp.float32),
                pltpu.VMEM(operators.shape, jnp.bfloat16),
                pltpu.VMEM((classes // quad * bins_all, quad * bins_all), jnp.bfloat16),
                pltpu.VMEM((half, classes // low_classes * bins_all, low_classes * 2 * ba_count), jnp.bfloat16),
                pltpu.SemaphoreType.DMA((5 + bins_dev,)),
                pltpu.SemaphoreType.DMA((2, half)),
                pltpu.SemaphoreType.DMA((2, half)),
                pltpu.SemaphoreType.DMA((2,)),
                pltpu.SemaphoreType.DMA((2,)),
                pltpu.SemaphoreType.DMA((2, half)),
                pltpu.SemaphoreType.DMA((2, half)),
                pltpu.SemaphoreType.DMA,
                pltpu.SemaphoreType.DMA((half,)),
            ],
            compiler_params=pltpu.CompilerParams(
                collective_id=0, has_side_effects=True, vmem_limit_bytes=16 * 2**20
            ),
        )(
            *[
                pltpu.with_memory_space_constraint(operand, pltpu.HBM)
                for operand in (
                    diffusivity,
                    density,
                    positions.reshape(1, remnants),
                    spectrum.T,
                    cell_class.reshape(cells, grid_z),
                    operators,
                )
            ]
        )
        return out.reshape(bins_all, planes, rows_y // ba_count, grid_z)

    in_specs = (P("ba", "gx", None, None), P("ba"), P(), P(None, "ba"), P("gx", "ba", None), P())
    return jax.shard_map(
        step, mesh=mesh, in_specs=in_specs, out_specs=P(None, "gx", "ba", None), check_vma=False
    )
```

```python
import functools

import jax
import jax.numpy as jnp
from jax import lax
from jax.experimental import pallas as pl
from jax.experimental.pallas import tpu as pltpu
from jax.sharding import PartitionSpec as P

MESH = pl.DeviceIdType.MESH

LOW = 0.1
STEPS = 32767.0
BIAS = 32768


def encode(rho):
    return ((rho - LOW) * STEPS + 0.5).astype(jnp.int32) - BIAS


def decode(code):
    return code.astype(jnp.int32).astype(jnp.float32) * (1.0 / STEPS) + (LOW + BIAS / STEPS)


def yz_sum(field):
    return (
        pltpu.roll(field, 1, 0)
        + pltpu.roll(field, field.shape[0] - 1, 0)
        + pltpu.roll(field, 1, 1)
        + pltpu.roll(field, field.shape[1] - 1, 1)
    )


def kernel(
    gx_count,
    ba_count,
    diff_hbm,
    density_ref,
    pos_hbm,
    spec_hbm,
    class_hbm,
    oper_ref,
    out_ref,
    diff_ref,
    pos_ref,
    spec_ref,
    class_ref,
    dens,
    stage,
    held,
    halo,
    parm_out,
    parm,
    source,
    rounded,
    gathered,
    wide,
    sums,
    opers,
    weights,
    chunk_weights,
    load_sem,
    swap_send,
    swap_recv,
    parm_send,
    parm_recv,
    halo_send,
    halo_recv,
    spread_send,
    spread_recv,
):
    bins_dev, planes, rows_y, grid_z = density_ref.shape
    half = bins_dev // 2
    ring = 2 * ba_count
    rows_dev = rows_y // ba_count
    bins_all = opers.shape[1]
    remnants = pos_ref.shape[1]
    part = remnants // 2
    gx = lax.axis_index("gx")
    ba = lax.axis_index("ba")
    side = lax.rem(gx, 2)
    column = gx - side
    me = side * ba_count + ba
    meet = lax.rem(ba + ba_count // 2, ba_count)
    right = lax.rem(gx + 2, gx_count)
    left = lax.rem(gx + gx_count - 2, gx_count)

    barrier = pltpu.get_barrier_semaphore()
    greetings = 0
    for chips in (0, 1, 2, ring // 2 - 2, ring // 2 - 1):
        for core in range(2):
            if chips or core:
                peer = 2 * lax.rem(me // 2 + chips, ring // 2) + lax.rem(me + core, 2)
                pl.semaphore_signal(
                    barrier,
                    inc=1,
                    device_id=(column + peer // ba_count, lax.rem(peer, ba_count)),
                    device_id_type=MESH,
                )
                greetings += 1
    for other in (left, right):
        pl.semaphore_signal(barrier, inc=1, device_id=(other, ba), device_id_type=MESH)
        greetings += 1

    loads = [
        pltpu.make_async_copy(diff_hbm, diff_ref, load_sem.at[0]),
        pltpu.make_async_copy(spec_hbm, spec_ref, load_sem.at[1]),
        pltpu.make_async_copy(pos_hbm, pos_ref, load_sem.at[2]),
        pltpu.make_async_copy(oper_ref, opers, load_sem.at[3]),
        pltpu.make_async_copy(class_hbm, class_ref, load_sem.at[4]),
    ]
    loads += [
        pltpu.make_async_copy(
            density_ref.at[h * half + b], dens.at[h * half + b], load_sem.at[5 + h * half + b]
        )
        for b in range(half)
        for h in range(2)
    ]
    for copy in loads[:2] + loads[5:] + loads[2:5]:
        copy.start()

    loads[0].wait()
    loads[1].wait()
    bin_row = lax.broadcasted_iota(jnp.int32, (half, grid_z), 0)
    for h in range(2):
        parm_out[h, :, 0:part] = spec_ref[
            h * half : (h + 1) * half, pl.ds(pl.multiple_of(side * part, part), part)
        ]
        value = jnp.zeros((half, grid_z), jnp.float32)
        for b in range(half):
            value = jnp.where(bin_row == b, diff_ref[h * half + b], value)
        parm_out[h, :, part:] = value
    swaps = []

    def encode_chunk(b):
        for h in range(2):
            loads[5 + 2 * b + h].wait()
            stage[h, b] = encode(dens[h * half + b]).astype(jnp.int16)

    def swap(b):
        for h in range(2):
            swaps.append(
                pltpu.make_async_remote_copy(
                    src_ref=stage.at[h, b],
                    dst_ref=held.at[side, b],
                    send_sem=swap_send.at[h, b],
                    recv_sem=swap_recv.at[side, b],
                    device_id=(column + h, meet),
                    device_id_type=MESH,
                )
            )
            swaps[-1].start()

    encode_chunk(0)
    pl.semaphore_wait(barrier, greetings)

    parms = []
    for h in range(2):
        target = (column + h, meet)
        parms.append(
            pltpu.make_async_remote_copy(
                src_ref=parm_out.at[h],
                dst_ref=parm.at[side],
                send_sem=parm_send.at[h],
                recv_sem=parm_recv.at[side],
                device_id=target,
                device_id_type=MESH,
            )
        )
        parms[h].start()
    swap(0)
    for b in range(1, half):
        encode_chunk(b)

    loads[2].wait()
    loads[3].wait()
    loads[4].wait()
    quad = weights.shape[1] // bins_all
    quads = weights.shape[0] // bins_all
    swap(1)

    planes_col = 2 * planes
    planes_src = planes_col + 2
    pos = pos_ref[...]
    pos_x = pos // (rows_y * grid_z)
    pos_y = lax.rem(pos // grid_z, rows_y)
    pos_z = lax.rem(pos, grid_z)
    width = gx_count * planes
    pos_x = lax.rem(pos_x + (width + 1) - column * planes, width)
    pos_row = pos_x * rows_y + pos_y
    is_row = lax.broadcasted_iota(jnp.int32, (planes_src * rows_y, remnants), 0) == pos_row
    is_row = jnp.where(is_row, 1.0, 0.0).astype(jnp.bfloat16)
    is_z = lax.broadcasted_iota(jnp.int32, (grid_z, remnants), 0) == pos_z
    swap(2)
    for s in range(2):
        pltpu.make_async_copy(parm.at[s], parm.at[s], parm_recv.at[s]).wait()
    swap(3)
    spec = jnp.concatenate([parm[0, :, 0:part], parm[1, :, 0:part]], axis=1)
    high = spec.astype(jnp.bfloat16).astype(jnp.float32)
    low = spec - high

    def inject(pair):
        total = jnp.zeros((planes_src * rows_y, 2 * grid_z), jnp.float32)
        for piece in (high, low):
            placed = [
                jnp.where(is_z, piece[b : b + 1], 0.0).astype(jnp.bfloat16)
                for b in (2 * pair, 2 * pair + 1)
            ]
            total += lax.dot_general(
                is_row,
                jnp.concatenate(placed, axis=0),
                (((1,), (1,)), ((), ())),
                preferred_element_type=jnp.float32,
            )
        for j in range(2):
            source[2 * pair + j] = total[:, j * grid_z : (j + 1) * grid_z].reshape(
                planes_src, rows_y, grid_z
            )

    halos = [[None, None] for _ in range(half)]

    def forward(b):
        for s in range(2):
            pltpu.make_async_copy(held.at[s, b], held.at[s, b], swap_recv.at[s, b]).wait()
            halos[b][s] = pltpu.make_async_remote_copy(
                src_ref=held.at[s, b],
                dst_ref=halo.at[s, b],
                send_sem=halo_send.at[s, b],
                recv_sem=halo_recv.at[s, b],
                device_id=(left if s == 0 else right, ba),
                device_id_type=MESH,
            )
            halos[b][s].start()

    low_classes = chunk_weights.shape[2] // ring
    high_classes = chunk_weights.shape[1] // bins_all

    def regroup():
        size = weights.shape[1]
        k = lax.broadcasted_iota(jnp.int32, (size, size), 0)
        n = lax.broadcasted_iota(jnp.int32, (size, size), 1)
        wanted = (n // bins_all) + half * lax.rem(n, ring)
        pick = (k // bins_all == lax.rem(n, bins_all) // ring) & (lax.rem(k, bins_all) == wanted)
        pick = jnp.where(pick, 1.0, 0.0).astype(jnp.bfloat16)
        per_high = low_classes // quad

        def one(a, carry):
            rows = pl.ds(pl.multiple_of(a * per_high * bins_all, bins_all), per_high * bins_all)
            picked = jnp.dot(weights[rows, :], pick, preferred_element_type=jnp.float32)
            picked = picked.astype(jnp.bfloat16)
            place = pl.ds(pl.multiple_of(a * bins_all, bins_all), bins_all)
            for b in range(half):
                chunk_weights[b, place, :] = jnp.concatenate(
                    [
                        picked[t * bins_all : (t + 1) * bins_all, b * bins_all : (b + 1) * bins_all]
                        for t in range(per_high)
                    ],
                    axis=1,
                )
            return carry

        lax.fori_loop(0, high_classes, one, 0)

    def diffuse(b):
        for s in range(2):
            halos[b][s].wait_recv()
        rate = parm[0, b : b + 1, part:]
        centre = 1.0 - 6.0 * rate
        fields = [decode(halo[1, b, p]) for p in range(planes)]
        fields += [decode(held[s, b, p]) for s in range(2) for p in range(planes)]
        fields += [decode(halo[0, b, p]) for p in range(planes)]
        sources = [source[b, p] for p in range(planes_src)]
        first = [
            centre * fields[p + 1] + rate * (fields[p] + fields[p + 2] + yz_sum(fields[p + 1])) + sources[p]
            for p in range(planes_src)
        ]
        second = [
            centre * first[p + 1]
            + rate * (first[p] + first[p + 2] + yz_sum(first[p + 1]))
            + sources[p + 1]
            for p in range(planes_col)
        ]
        for s in range(2):
            block = jnp.concatenate(
                [second[s * planes + p].reshape(ba_count, rows_dev, grid_z) for p in range(planes)],
                axis=1,
            )
            rounded[b, pl.ds(s * ba_count, ba_count)] = block.astype(jnp.bfloat16)

    group = 2 * meet + side
    peers = []
    for offset in sorted(range(1, ring), key=lambda o: -min(o, ring - o)):
        peer = lax.rem(me + offset, ring)
        peers.append((peer, (column + peer // ba_count, lax.rem(peer, ba_count))))

    def spread(b):
        slot = gathered.at[b, group]
        for peer, place in peers:
            pltpu.make_async_remote_copy(
                src_ref=rounded.at[b, peer],
                dst_ref=slot,
                send_sem=spread_send,
                recv_sem=spread_recv.at[b],
                device_id=place,
                device_id_type=MESH,
            ).start()
        pltpu.make_async_copy(rounded.at[b, me], slot, spread_recv.at[b]).start()

    inject(0)
    forward(0)
    inject(1)
    forward(1)
    forward(2)
    forward(3)
    diffuse(0)
    spread(0)
    diffuse(1)
    spread(1)
    diffuse(2)
    spread(2)
    diffuse(3)
    spread(3)

    def arrange(a, carry):
        weights[pl.ds(pl.multiple_of(a * bins_all, bins_all), bins_all), :] = jnp.concatenate(
            [opers[a * quad + j] for j in range(quad)], axis=1
        )
        return carry

    lax.fori_loop(0, quads, arrange, 0, unroll=4)
    regroup()

    cells = planes * rows_dev

    def update(b):
        pltpu.make_async_copy(gathered.at[b], gathered.at[b], spread_recv.at[b]).wait()
        wide[...] = gathered[b].astype(jnp.float32).reshape(wide.shape)

        def pair(step, carry):
            first_row = 2 * step
            values = jnp.concatenate(
                [wide[pl.ds(first_row + j, ring, stride=cells), :] for j in range(2)], axis=1
            )
            classes = jnp.concatenate(
                [class_ref[pl.ds(first_row + j, 1), :] for j in range(2)], axis=1
            )
            low_class = lax.rem(classes, low_classes)
            high_class = classes // low_classes
            stacked = jnp.concatenate(
                [jnp.where(low_class == j, values, 0.0) for j in range(low_classes)], axis=0
            ).astype(jnp.bfloat16)
            products = jnp.dot(chunk_weights[b], stacked, preferred_element_type=jnp.float32)
            result = products[0:bins_all]
            for a in range(1, high_classes):
                result = jnp.where(
                    high_class == a, products[a * bins_all : (a + 1) * bins_all], result
                )
            if b > 0:
                result += sums[step]
            if b < half - 1:
                sums[step] = result
            else:
                for j in range(2):
                    out_ref[pl.ds(first_row + j, bins_all, stride=cells), :] = result[
                        :, j * grid_z : (j + 1) * grid_z
                    ]
            return carry

        lax.fori_loop(0, cells // 2, pair, 0, unroll=8)

    for b in range(half):
        update(b)

    for copy in parms + swaps:
        copy.wait_send()
    for b in range(half):
        for s in range(2):
            halos[b][s].wait_send()
    sent = rounded.at[:, pl.ds(0, ring - 1)]
    pltpu.make_async_copy(sent, sent, spread_send).wait()


def solution(mesh):
    gx_count, ba_count = mesh.shape["gx"], mesh.shape["ba"]

    def step(density, diffusivity, positions, spectrum, cell_class, operators):
        bins_dev, planes, rows_y, grid_z = density.shape
        classes, bins_all, _ = operators.shape
        remnants = positions.shape[0]
        half = bins_dev // 2
        cells = planes * (rows_y // ba_count)
        quad, low_classes = 4, 16
        vmem = pl.BlockSpec(memory_space=pltpu.VMEM)
        out = pl.pallas_call(
            functools.partial(kernel, gx_count, ba_count),
            out_shape=jax.ShapeDtypeStruct((bins_all * cells, grid_z), jnp.float32),
            in_specs=[pl.BlockSpec(memory_space=pltpu.HBM)] * 6,
            out_specs=vmem,
            scratch_shapes=[
                pltpu.SMEM((bins_dev,), jnp.float32),
                pltpu.VMEM((1, remnants), jnp.int32),
                pltpu.VMEM((bins_dev, remnants), jnp.float32),
                pltpu.VMEM((cells, grid_z), jnp.int32),
                pltpu.VMEM(density.shape, jnp.float32),
                pltpu.VMEM((2, half, planes, rows_y, grid_z), jnp.int16),
                pltpu.VMEM((2, half, planes, rows_y, grid_z), jnp.int16),
                pltpu.VMEM((2, half, planes, rows_y, grid_z), jnp.int16),
                pltpu.VMEM((2, half, remnants // 2 + grid_z), jnp.float32),
                pltpu.VMEM((2, half, remnants // 2 + grid_z), jnp.float32),
                pltpu.VMEM((half, 2 * planes + 2, rows_y, grid_z), jnp.float32),
                pltpu.VMEM((half, 2 * ba_count, cells, grid_z), jnp.bfloat16),
                pltpu.VMEM((half, 2 * ba_count, cells, grid_z), jnp.bfloat16),
                pltpu.VMEM((2 * ba_count * cells, grid_z), jnp.float32),
                pltpu.VMEM((cells // 2, bins_all, 2 * grid_z), jnp.float32),
                pltpu.VMEM(operators.shape, jnp.bfloat16),
                pltpu.VMEM((classes // quad * bins_all, quad * bins_all), jnp.bfloat16),
                pltpu.VMEM((half, classes // low_classes * bins_all, low_classes * 2 * ba_count), jnp.bfloat16),
                pltpu.SemaphoreType.DMA((5 + bins_dev,)),
                pltpu.SemaphoreType.DMA((2, half)),
                pltpu.SemaphoreType.DMA((2, half)),
                pltpu.SemaphoreType.DMA((2,)),
                pltpu.SemaphoreType.DMA((2,)),
                pltpu.SemaphoreType.DMA((2, half)),
                pltpu.SemaphoreType.DMA((2, half)),
                pltpu.SemaphoreType.DMA,
                pltpu.SemaphoreType.DMA((half,)),
            ],
            compiler_params=pltpu.CompilerParams(
                collective_id=0, has_side_effects=True, vmem_limit_bytes=16 * 2**20
            ),
        )(
            *[
                pltpu.with_memory_space_constraint(operand, pltpu.HBM)
                for operand in (
                    diffusivity,
                    density,
                    positions.reshape(1, remnants),
                    spectrum.T,
                    cell_class.reshape(cells, grid_z),
                    operators,
                )
            ]
        )
        return out.reshape(bins_all, planes, rows_y // ba_count, grid_z)

    in_specs = (P("ba", "gx", None, None), P("ba"), P(), P(None, "ba"), P("gx", "ba", None), P())
    return jax.shard_map(
        step, mesh=mesh, in_specs=in_specs, out_specs=P(None, "gx", "ba", None), check_vma=False
    )
```

```python
import functools

import jax
import jax.numpy as jnp
from jax import lax
from jax.experimental import pallas as pl
from jax.experimental.pallas import tpu as pltpu
from jax.sharding import PartitionSpec as P

MESH = pl.DeviceIdType.MESH

LOW = 0.1
STEPS = 32767.0
BIAS = 32768


def encode(rho):
    return ((rho - LOW) * STEPS + 0.5).astype(jnp.int32) - BIAS


def decode(code):
    return code.astype(jnp.int32).astype(jnp.float32) * (1.0 / STEPS) + (LOW + BIAS / STEPS)


def yz_sum(field):
    return (
        pltpu.roll(field, 1, 0)
        + pltpu.roll(field, field.shape[0] - 1, 0)
        + pltpu.roll(field, 1, 1)
        + pltpu.roll(field, field.shape[1] - 1, 1)
    )


def kernel(
    gx_count,
    ba_count,
    diff_hbm,
    density_ref,
    pos_hbm,
    spec_hbm,
    class_hbm,
    oper_ref,
    out_ref,
    diff_ref,
    pos_ref,
    spec_ref,
    class_ref,
    dens,
    stage,
    held,
    halo,
    parm_out,
    parm,
    source,
    inner,
    rounded,
    gathered,
    wide,
    sums,
    opers,
    weights,
    chunk_weights,
    load_sem,
    swap_send,
    swap_recv,
    parm_send,
    parm_recv,
    halo_send,
    halo_recv,
    spread_send,
    spread_recv,
):
    bins_dev, planes, rows_y, grid_z = density_ref.shape
    half = bins_dev // 2
    ring = 2 * ba_count
    rows_dev = rows_y // ba_count
    bins_all = opers.shape[1]
    remnants = pos_ref.shape[1]
    part = remnants // 2
    gx = lax.axis_index("gx")
    ba = lax.axis_index("ba")
    side = lax.rem(gx, 2)
    column = gx - side
    me = side * ba_count + ba
    meet = lax.rem(ba + ba_count // 2, ba_count)
    right = lax.rem(gx + 2, gx_count)
    left = lax.rem(gx + gx_count - 2, gx_count)

    barrier = pltpu.get_barrier_semaphore()
    greetings = 0
    for chips in (0, 1, 2, ring // 2 - 2, ring // 2 - 1):
        for core in range(2):
            if chips or core:
                peer = 2 * lax.rem(me // 2 + chips, ring // 2) + lax.rem(me + core, 2)
                pl.semaphore_signal(
                    barrier,
                    inc=1,
                    device_id=(column + peer // ba_count, lax.rem(peer, ba_count)),
                    device_id_type=MESH,
                )
                greetings += 1
    for other in (left, right):
        pl.semaphore_signal(barrier, inc=1, device_id=(other, ba), device_id_type=MESH)
        greetings += 1

    loads = [
        pltpu.make_async_copy(diff_hbm, diff_ref, load_sem.at[0]),
        pltpu.make_async_copy(spec_hbm, spec_ref, load_sem.at[1]),
        pltpu.make_async_copy(pos_hbm, pos_ref, load_sem.at[2]),
        pltpu.make_async_copy(oper_ref, opers, load_sem.at[3]),
        pltpu.make_async_copy(class_hbm, class_ref, load_sem.at[4]),
    ]
    loads += [
        pltpu.make_async_copy(
            density_ref.at[h * half + b], dens.at[h * half + b], load_sem.at[5 + h * half + b]
        )
        for b in range(half)
        for h in range(2)
    ]
    for copy in loads[:2] + loads[5:] + loads[2:5]:
        copy.start()

    loads[0].wait()
    loads[1].wait()
    bin_row = lax.broadcasted_iota(jnp.int32, (half, grid_z), 0)
    for h in range(2):
        parm_out[h, :, 0:part] = spec_ref[
            h * half : (h + 1) * half, pl.ds(pl.multiple_of(side * part, part), part)
        ]
        value = jnp.zeros((half, grid_z), jnp.float32)
        for b in range(half):
            value = jnp.where(bin_row == b, diff_ref[h * half + b], value)
        parm_out[h, :, part:] = value
    swaps = []

    def encode_chunk(b):
        for h in range(2):
            loads[5 + 2 * b + h].wait()
            stage[h, b] = encode(dens[h * half + b]).astype(jnp.int16)

    def swap(b):
        for h in range(2):
            swaps.append(
                pltpu.make_async_remote_copy(
                    src_ref=stage.at[h, b],
                    dst_ref=held.at[side, b],
                    send_sem=swap_send.at[h, b],
                    recv_sem=swap_recv.at[side, b],
                    device_id=(column + h, meet),
                    device_id_type=MESH,
                )
            )
            swaps[-1].start()

    encode_chunk(0)
    pl.semaphore_wait(barrier, greetings)

    parms = []
    for h in range(2):
        target = (column + h, meet)
        parms.append(
            pltpu.make_async_remote_copy(
                src_ref=parm_out.at[h],
                dst_ref=parm.at[side],
                send_sem=parm_send.at[h],
                recv_sem=parm_recv.at[side],
                device_id=target,
                device_id_type=MESH,
            )
        )
        parms[h].start()
    swap(0)
    for b in range(1, half):
        encode_chunk(b)

    loads[2].wait()
    loads[3].wait()
    loads[4].wait()
    quad = weights.shape[1] // bins_all
    quads = weights.shape[0] // bins_all
    swap(1)

    planes_col = 2 * planes
    planes_src = planes_col + 2
    pos = pos_ref[...]
    pos_x = pos // (rows_y * grid_z)
    pos_y = lax.rem(pos // grid_z, rows_y)
    pos_z = lax.rem(pos, grid_z)
    width = gx_count * planes
    pos_x = lax.rem(pos_x + (width + 1) - column * planes, width)
    pos_row = pos_x * rows_y + pos_y
    is_row = lax.broadcasted_iota(jnp.int32, (planes_src * rows_y, remnants), 0) == pos_row
    is_row = jnp.where(is_row, 1.0, 0.0).astype(jnp.bfloat16)
    is_z = lax.broadcasted_iota(jnp.int32, (grid_z, remnants), 0) == pos_z
    swap(2)
    for s in range(2):
        pltpu.make_async_copy(parm.at[s], parm.at[s], parm_recv.at[s]).wait()
    swap(3)
    spec = jnp.concatenate([parm[0, :, 0:part], parm[1, :, 0:part]], axis=1)
    high = spec.astype(jnp.bfloat16).astype(jnp.float32)
    low = spec - high

    def inject(pair):
        total = jnp.zeros((planes_src * rows_y, 2 * grid_z), jnp.float32)
        for piece in (high, low):
            placed = [
                jnp.where(is_z, piece[b : b + 1], 0.0).astype(jnp.bfloat16)
                for b in (2 * pair, 2 * pair + 1)
            ]
            total += lax.dot_general(
                is_row,
                jnp.concatenate(placed, axis=0),
                (((1,), (1,)), ((), ())),
                preferred_element_type=jnp.float32,
            )
        for j in range(2):
            source[2 * pair + j] = total[:, j * grid_z : (j + 1) * grid_z].reshape(
                planes_src, rows_y, grid_z
            )

    halos = [[None, None] for _ in range(half)]

    def forward(b):
        for s in range(2):
            pltpu.make_async_copy(held.at[s, b], held.at[s, b], swap_recv.at[s, b]).wait()
            halos[b][s] = pltpu.make_async_remote_copy(
                src_ref=held.at[s, b],
                dst_ref=halo.at[s, b],
                send_sem=halo_send.at[s, b],
                recv_sem=halo_recv.at[s, b],
                device_id=(left if s == 0 else right, ba),
                device_id_type=MESH,
            )
            halos[b][s].start()

    low_classes = chunk_weights.shape[2] // ring
    high_classes = chunk_weights.shape[1] // bins_all

    def regroup():
        size = weights.shape[1]
        k = lax.broadcasted_iota(jnp.int32, (size, size), 0)
        n = lax.broadcasted_iota(jnp.int32, (size, size), 1)
        wanted = (n // bins_all) + half * lax.rem(n, ring)
        pick = (k // bins_all == lax.rem(n, bins_all) // ring) & (lax.rem(k, bins_all) == wanted)
        pick = jnp.where(pick, 1.0, 0.0).astype(jnp.bfloat16)
        per_high = low_classes // quad

        def one(a, carry):
            rows = pl.ds(pl.multiple_of(a * per_high * bins_all, bins_all), per_high * bins_all)
            picked = jnp.dot(weights[rows, :], pick, preferred_element_type=jnp.float32)
            picked = picked.astype(jnp.bfloat16)
            place = pl.ds(pl.multiple_of(a * bins_all, bins_all), bins_all)
            for b in range(half):
                chunk_weights[b, place, :] = jnp.concatenate(
                    [
                        picked[t * bins_all : (t + 1) * bins_all, b * bins_all : (b + 1) * bins_all]
                        for t in range(per_high)
                    ],
                    axis=1,
                )
            return carry

        lax.fori_loop(0, high_classes, one, 0)

    def prepare(b):
        rate = parm[0, b : b + 1, part:]
        centre = 1.0 - 6.0 * rate
        fields = [decode(held[s, b, p]) for s in range(2) for p in range(planes)]
        for p in range(planes_col):
            around = yz_sum(fields[p])
            if p > 0:
                around += fields[p - 1]
            if p + 1 < planes_col:
                around += fields[p + 1]
            inner[b, p] = centre * fields[p] + rate * around + source[b, p + 1]

    def diffuse(b):
        for s in range(2):
            halos[b][s].wait_recv()
        rate = parm[0, b : b + 1, part:]
        centre = 1.0 - 6.0 * rate
        before = [decode(halo[1, b, p]) for p in range(planes)]
        after = [decode(halo[0, b, p]) for p in range(planes)]
        sources = [source[b, p] for p in range(planes_src)]
        first = [
            centre * before[-1]
            + rate * (before[-2] + decode(held[0, b, 0]) + yz_sum(before[-1]))
            + sources[0]
        ]
        first += [inner[b, p] for p in range(planes_col)]
        first[1] += rate * before[-1]
        first[planes_col] += rate * after[0]
        first.append(
            centre * after[0]
            + rate * (decode(held[1, b, planes - 1]) + after[1] + yz_sum(after[0]))
            + sources[planes_src - 1]
        )
        second = [
            centre * first[p + 1]
            + rate * (first[p] + first[p + 2] + yz_sum(first[p + 1]))
            + sources[p + 1]
            for p in range(planes_col)
        ]
        for s in range(2):
            block = jnp.concatenate(
                [second[s * planes + p].reshape(ba_count, rows_dev, grid_z) for p in range(planes)],
                axis=1,
            )
            rounded[b, pl.ds(s * ba_count, ba_count)] = block.astype(jnp.bfloat16)

    group = 2 * meet + side
    peers = []
    for offset in sorted(range(1, ring), key=lambda o: -min(o, ring - o)):
        peer = lax.rem(me + offset, ring)
        peers.append((peer, (column + peer // ba_count, lax.rem(peer, ba_count))))

    def spread(b):
        slot = gathered.at[b, group]
        for peer, place in peers:
            pltpu.make_async_remote_copy(
                src_ref=rounded.at[b, peer],
                dst_ref=slot,
                send_sem=spread_send,
                recv_sem=spread_recv.at[b],
                device_id=place,
                device_id_type=MESH,
            ).start()
        pltpu.make_async_copy(rounded.at[b, me], slot, spread_recv.at[b]).start()

    inject(0)
    forward(0)
    prepare(0)
    inject(1)
    forward(1)
    prepare(1)
    forward(2)
    prepare(2)
    forward(3)
    prepare(3)
    diffuse(0)
    spread(0)
    diffuse(1)
    spread(1)
    diffuse(2)
    spread(2)
    diffuse(3)
    spread(3)

    def arrange(a, carry):
        weights[pl.ds(pl.multiple_of(a * bins_all, bins_all), bins_all), :] = jnp.concatenate(
            [opers[a * quad + j] for j in range(quad)], axis=1
        )
        return carry

    lax.fori_loop(0, quads, arrange, 0, unroll=4)
    regroup()

    cells = planes * rows_dev

    def update(b):
        pltpu.make_async_copy(gathered.at[b], gathered.at[b], spread_recv.at[b]).wait()
        wide[...] = gathered[b].astype(jnp.float32).reshape(wide.shape)

        def pair(step, carry):
            first_row = 2 * step
            values = jnp.concatenate(
                [wide[pl.ds(first_row + j, ring, stride=cells), :] for j in range(2)], axis=1
            )
            classes = jnp.concatenate(
                [class_ref[pl.ds(first_row + j, 1), :] for j in range(2)], axis=1
            )
            low_class = lax.rem(classes, low_classes)
            high_class = classes // low_classes
            stacked = jnp.concatenate(
                [jnp.where(low_class == j, values, 0.0) for j in range(low_classes)], axis=0
            ).astype(jnp.bfloat16)
            products = jnp.dot(chunk_weights[b], stacked, preferred_element_type=jnp.float32)
            result = products[0:bins_all]
            for a in range(1, high_classes):
                result = jnp.where(
                    high_class == a, products[a * bins_all : (a + 1) * bins_all], result
                )
            if b > 0:
                result += sums[step]
            if b < half - 1:
                sums[step] = result
            else:
                for j in range(2):
                    out_ref[pl.ds(first_row + j, bins_all, stride=cells), :] = result[
                        :, j * grid_z : (j + 1) * grid_z
                    ]
            return carry

        lax.fori_loop(0, cells // 2, pair, 0, unroll=8)

    for b in range(half):
        update(b)

    for copy in parms + swaps:
        copy.wait_send()
    for b in range(half):
        for s in range(2):
            halos[b][s].wait_send()
    sent = rounded.at[:, pl.ds(0, ring - 1)]
    pltpu.make_async_copy(sent, sent, spread_send).wait()


def solution(mesh):
    gx_count, ba_count = mesh.shape["gx"], mesh.shape["ba"]

    def step(density, diffusivity, positions, spectrum, cell_class, operators):
        bins_dev, planes, rows_y, grid_z = density.shape
        classes, bins_all, _ = operators.shape
        remnants = positions.shape[0]
        half = bins_dev // 2
        cells = planes * (rows_y // ba_count)
        quad, low_classes = 4, 16
        vmem = pl.BlockSpec(memory_space=pltpu.VMEM)
        out = pl.pallas_call(
            functools.partial(kernel, gx_count, ba_count),
            out_shape=jax.ShapeDtypeStruct((bins_all * cells, grid_z), jnp.float32),
            in_specs=[pl.BlockSpec(memory_space=pltpu.HBM)] * 6,
            out_specs=vmem,
            scratch_shapes=[
                pltpu.SMEM((bins_dev,), jnp.float32),
                pltpu.VMEM((1, remnants), jnp.int32),
                pltpu.VMEM((bins_dev, remnants), jnp.float32),
                pltpu.VMEM((cells, grid_z), jnp.int32),
                pltpu.VMEM(density.shape, jnp.float32),
                pltpu.VMEM((2, half, planes, rows_y, grid_z), jnp.int16),
                pltpu.VMEM((2, half, planes, rows_y, grid_z), jnp.int16),
                pltpu.VMEM((2, half, planes, rows_y, grid_z), jnp.int16),
                pltpu.VMEM((2, half, remnants // 2 + grid_z), jnp.float32),
                pltpu.VMEM((2, half, remnants // 2 + grid_z), jnp.float32),
                pltpu.VMEM((half, 2 * planes + 2, rows_y, grid_z), jnp.float32),
                pltpu.VMEM((half, 2 * planes, rows_y, grid_z), jnp.float32),
                pltpu.VMEM((half, 2 * ba_count, cells, grid_z), jnp.bfloat16),
                pltpu.VMEM((half, 2 * ba_count, cells, grid_z), jnp.bfloat16),
                pltpu.VMEM((2 * ba_count * cells, grid_z), jnp.float32),
                pltpu.VMEM((cells // 2, bins_all, 2 * grid_z), jnp.float32),
                pltpu.VMEM(operators.shape, jnp.bfloat16),
                pltpu.VMEM((classes // quad * bins_all, quad * bins_all), jnp.bfloat16),
                pltpu.VMEM((half, classes // low_classes * bins_all, low_classes * 2 * ba_count), jnp.bfloat16),
                pltpu.SemaphoreType.DMA((5 + bins_dev,)),
                pltpu.SemaphoreType.DMA((2, half)),
                pltpu.SemaphoreType.DMA((2, half)),
                pltpu.SemaphoreType.DMA((2,)),
                pltpu.SemaphoreType.DMA((2,)),
                pltpu.SemaphoreType.DMA((2, half)),
                pltpu.SemaphoreType.DMA((2, half)),
                pltpu.SemaphoreType.DMA,
                pltpu.SemaphoreType.DMA((half,)),
            ],
            compiler_params=pltpu.CompilerParams(
                collective_id=0, has_side_effects=True, vmem_limit_bytes=16 * 2**20
            ),
        )(
            *[
                pltpu.with_memory_space_constraint(operand, pltpu.HBM)
                for operand in (
                    diffusivity,
                    density,
                    positions.reshape(1, remnants),
                    spectrum.T,
                    cell_class.reshape(cells, grid_z),
                    operators,
                )
            ]
        )
        return out.reshape(bins_all, planes, rows_y // ba_count, grid_z)

    in_specs = (P("ba", "gx", None, None), P("ba"), P(), P(None, "ba"), P("gx", "ba", None), P())
    return jax.shard_map(
        step, mesh=mesh, in_specs=in_specs, out_specs=P(None, "gx", "ba", None), check_vma=False
    )
```

```python
import functools

import jax
import jax.numpy as jnp
from jax import lax
from jax.experimental import pallas as pl
from jax.experimental.pallas import tpu as pltpu
from jax.sharding import PartitionSpec as P

MESH = pl.DeviceIdType.MESH

LOW = 0.1
STEPS = 32767.0
BIAS = 32768


def encode(rho):
    return ((rho - LOW) * STEPS + 0.5).astype(jnp.int32) - BIAS


def decode(code):
    return code.astype(jnp.int32).astype(jnp.float32) * (1.0 / STEPS) + (LOW + BIAS / STEPS)


def yz_sum(field):
    return (
        pltpu.roll(field, 1, 0)
        + pltpu.roll(field, field.shape[0] - 1, 0)
        + pltpu.roll(field, 1, 1)
        + pltpu.roll(field, field.shape[1] - 1, 1)
    )


def kernel(
    gx_count,
    ba_count,
    diff_hbm,
    density_ref,
    pos_hbm,
    spec_hbm,
    class_hbm,
    oper_ref,
    out_ref,
    diff_ref,
    pos_ref,
    spec_ref,
    class_ref,
    dens,
    stage,
    held,
    halo,
    parm_out,
    parm,
    source,
    inner,
    rounded,
    gathered,
    wide,
    sums,
    opers,
    weights,
    chunk_weights,
    load_sem,
    swap_send,
    swap_recv,
    parm_send,
    parm_recv,
    halo_send,
    halo_recv,
    spread_send,
    spread_recv,
):
    bins_dev, planes, rows_y, grid_z = density_ref.shape
    half = bins_dev // 2
    ring = 2 * ba_count
    rows_dev = rows_y // ba_count
    bins_all = opers.shape[1]
    remnants = pos_ref.shape[1]
    part = remnants // 2
    gx = lax.axis_index("gx")
    ba = lax.axis_index("ba")
    side = lax.rem(gx, 2)
    column = gx - side
    me = side * ba_count + ba
    meet = lax.rem(ba + ba_count // 2, ba_count)
    right = lax.rem(gx + 2, gx_count)
    left = lax.rem(gx + gx_count - 2, gx_count)

    barrier = pltpu.get_barrier_semaphore()
    greetings = 0
    for chips in (0, 1, 2, ring // 2 - 2, ring // 2 - 1):
        for core in range(2):
            if chips or core:
                peer = 2 * lax.rem(me // 2 + chips, ring // 2) + lax.rem(me + core, 2)
                pl.semaphore_signal(
                    barrier,
                    inc=1,
                    device_id=(column + peer // ba_count, lax.rem(peer, ba_count)),
                    device_id_type=MESH,
                )
                greetings += 1
    for other in (left, right):
        pl.semaphore_signal(barrier, inc=1, device_id=(other, ba), device_id_type=MESH)
        greetings += 1

    loads = [
        pltpu.make_async_copy(diff_hbm, diff_ref, load_sem.at[0]),
        pltpu.make_async_copy(spec_hbm, spec_ref, load_sem.at[1]),
        pltpu.make_async_copy(pos_hbm, pos_ref, load_sem.at[2]),
        pltpu.make_async_copy(oper_ref, opers, load_sem.at[3]),
        pltpu.make_async_copy(class_hbm, class_ref, load_sem.at[4]),
    ]
    loads += [
        pltpu.make_async_copy(
            density_ref.at[h * half + b], dens.at[h * half + b], load_sem.at[5 + h * half + b]
        )
        for b in range(half)
        for h in range(2)
    ]
    for copy in loads[:2] + loads[5:] + loads[2:5]:
        copy.start()

    loads[0].wait()
    loads[1].wait()
    bin_row = lax.broadcasted_iota(jnp.int32, (half, grid_z), 0)
    for h in range(2):
        parm_out[h, :, 0:part] = spec_ref[
            h * half : (h + 1) * half, pl.ds(pl.multiple_of(side * part, part), part)
        ]
        value = jnp.zeros((half, grid_z), jnp.float32)
        for b in range(half):
            value = jnp.where(bin_row == b, diff_ref[h * half + b], value)
        parm_out[h, :, part:] = value
    swaps = []

    def encode_chunk(b):
        for h in range(2):
            loads[5 + 2 * b + h].wait()
            stage[h, b] = encode(dens[h * half + b]).astype(jnp.int16)

    def swap(b):
        for h in range(2):
            swaps.append(
                pltpu.make_async_remote_copy(
                    src_ref=stage.at[h, b],
                    dst_ref=held.at[side, b],
                    send_sem=swap_send.at[h, b],
                    recv_sem=swap_recv.at[side, b],
                    device_id=(column + h, meet),
                    device_id_type=MESH,
                )
            )
            swaps[-1].start()

    encode_chunk(0)
    pl.semaphore_wait(barrier, greetings)

    parms = []
    for h in range(2):
        target = (column + h, meet)
        parms.append(
            pltpu.make_async_remote_copy(
                src_ref=parm_out.at[h],
                dst_ref=parm.at[side],
                send_sem=parm_send.at[h],
                recv_sem=parm_recv.at[side],
                device_id=target,
                device_id_type=MESH,
            )
        )
        parms[h].start()
    swap(0)
    for b in range(1, half):
        encode_chunk(b)

    loads[2].wait()
    loads[3].wait()
    loads[4].wait()
    quad = weights.shape[1] // bins_all
    quads = weights.shape[0] // bins_all
    swap(1)

    planes_col = 2 * planes
    planes_src = planes_col + 2
    pos = pos_ref[...]
    pos_x = pos // (rows_y * grid_z)
    pos_y = lax.rem(pos // grid_z, rows_y)
    pos_z = lax.rem(pos, grid_z)
    width = gx_count * planes
    pos_x = lax.rem(pos_x + (width + 1) - column * planes, width)
    pos_row = pos_x * rows_y + pos_y
    is_row = lax.broadcasted_iota(jnp.int32, (planes_src * rows_y, remnants), 0) == pos_row
    is_row = jnp.where(is_row, 1.0, 0.0).astype(jnp.bfloat16)
    is_z = lax.broadcasted_iota(jnp.int32, (grid_z, remnants), 0) == pos_z
    swap(2)
    for s in range(2):
        pltpu.make_async_copy(parm.at[s], parm.at[s], parm_recv.at[s]).wait()
    swap(3)
    spec = jnp.concatenate([parm[0, :, 0:part], parm[1, :, 0:part]], axis=1)
    high = spec.astype(jnp.bfloat16).astype(jnp.float32)
    low = spec - high

    def inject(pair):
        total = jnp.zeros((planes_src * rows_y, 2 * grid_z), jnp.float32)
        for piece in (high, low):
            placed = [
                jnp.where(is_z, piece[b : b + 1], 0.0).astype(jnp.bfloat16)
                for b in (2 * pair, 2 * pair + 1)
            ]
            total += lax.dot_general(
                is_row,
                jnp.concatenate(placed, axis=0),
                (((1,), (1,)), ((), ())),
                preferred_element_type=jnp.float32,
            )
        for j in range(2):
            source[2 * pair + j] = total[:, j * grid_z : (j + 1) * grid_z].reshape(
                planes_src, rows_y, grid_z
            )

    halos = [[None, None] for _ in range(half)]

    def forward(b):
        for s in range(2):
            pltpu.make_async_copy(held.at[s, b], held.at[s, b], swap_recv.at[s, b]).wait()
            halos[b][s] = pltpu.make_async_remote_copy(
                src_ref=held.at[s, b],
                dst_ref=halo.at[s, b],
                send_sem=halo_send.at[s, b],
                recv_sem=halo_recv.at[s, b],
                device_id=(left if s == 0 else right, ba),
                device_id_type=MESH,
            )
            halos[b][s].start()

    low_classes = chunk_weights.shape[2] // ring
    high_classes = chunk_weights.shape[1] // bins_all

    def regroup():
        size = weights.shape[1]
        k = lax.broadcasted_iota(jnp.int32, (size, size), 0)
        n = lax.broadcasted_iota(jnp.int32, (size, size), 1)
        wanted = (n // bins_all) + half * lax.rem(n, ring)
        pick = (k // bins_all == lax.rem(n, bins_all) // ring) & (lax.rem(k, bins_all) == wanted)
        pick = jnp.where(pick, 1.0, 0.0).astype(jnp.bfloat16)
        per_high = low_classes // quad

        def one(a, carry):
            rows = pl.ds(pl.multiple_of(a * per_high * bins_all, bins_all), per_high * bins_all)
            picked = jnp.dot(weights[rows, :], pick, preferred_element_type=jnp.float32)
            picked = picked.astype(jnp.bfloat16)
            place = pl.ds(pl.multiple_of(a * bins_all, bins_all), bins_all)
            for b in range(half):
                chunk_weights[b, place, :] = jnp.concatenate(
                    [
                        picked[t * bins_all : (t + 1) * bins_all, b * bins_all : (b + 1) * bins_all]
                        for t in range(per_high)
                    ],
                    axis=1,
                )
            return carry

        lax.fori_loop(0, high_classes, one, 0)

    def prepare(b):
        rate = parm[0, b : b + 1, part:]
        centre = 1.0 - 6.0 * rate
        fields = [decode(held[s, b, p]) for s in range(2) for p in range(planes)]
        for p in range(planes_col):
            around = yz_sum(fields[p])
            if p > 0:
                around += fields[p - 1]
            if p + 1 < planes_col:
                around += fields[p + 1]
            inner[b, p] = centre * fields[p] + rate * around + source[b, p + 1]

    def diffuse(b):
        for s in range(2):
            halos[b][s].wait_recv()
        rate = parm[0, b : b + 1, part:]
        centre = 1.0 - 6.0 * rate
        before = [decode(halo[1, b, p]) for p in range(planes)]
        after = [decode(halo[0, b, p]) for p in range(planes)]
        sources = [source[b, p] for p in range(planes_src)]
        first = [
            centre * before[-1]
            + rate * (before[-2] + decode(held[0, b, 0]) + yz_sum(before[-1]))
            + sources[0]
        ]
        first += [inner[b, p] for p in range(planes_col)]
        first[1] += rate * before[-1]
        first[planes_col] += rate * after[0]
        first.append(
            centre * after[0]
            + rate * (decode(held[1, b, planes - 1]) + after[1] + yz_sum(after[0]))
            + sources[planes_src - 1]
        )
        second = [
            centre * first[p + 1]
            + rate * (first[p] + first[p + 2] + yz_sum(first[p + 1]))
            + sources[p + 1]
            for p in range(planes_col)
        ]
        for s in range(2):
            block = jnp.concatenate(
                [second[s * planes + p].reshape(ba_count, rows_dev, grid_z) for p in range(planes)],
                axis=1,
            )
            rounded[b, pl.ds(s * ba_count, ba_count)] = block.astype(jnp.bfloat16)

    group = 2 * meet + side
    peers = []
    for offset in sorted(range(1, ring), key=lambda o: -min(o, ring - o)):
        peer = lax.rem(me + offset, ring)
        peers.append((peer, (column + peer // ba_count, lax.rem(peer, ba_count))))

    def spread(b):
        slot = gathered.at[b, group]
        for peer, place in peers:
            pltpu.make_async_remote_copy(
                src_ref=rounded.at[b, peer],
                dst_ref=slot,
                send_sem=spread_send,
                recv_sem=spread_recv.at[b],
                device_id=place,
                device_id_type=MESH,
            ).start()
        pltpu.make_async_copy(rounded.at[b, me], slot, spread_recv.at[b]).start()

    inject(0)
    forward(0)
    prepare(0)
    inject(1)
    forward(1)
    prepare(1)
    forward(2)
    prepare(2)
    forward(3)
    prepare(3)
    diffuse(0)
    spread(0)
    diffuse(1)
    spread(1)
    diffuse(2)
    spread(2)
    diffuse(3)
    spread(3)

    def arrange(a, carry):
        weights[pl.ds(pl.multiple_of(a * bins_all, bins_all), bins_all), :] = jnp.concatenate(
            [opers[a * quad + j] for j in range(quad)], axis=1
        )
        return carry

    lax.fori_loop(0, quads, arrange, 0, unroll=4)
    regroup()

    cells = planes * rows_dev

    def update(b):
        pltpu.make_async_copy(gathered.at[b], gathered.at[b], spread_recv.at[b]).wait()
        wide[...] = gathered[b].astype(jnp.float32).reshape(wide.shape)

        def pair(step, carry):
            first_row = 2 * step
            values = jnp.concatenate(
                [wide[pl.ds(first_row + j, ring, stride=cells), :] for j in range(2)], axis=1
            )
            classes = jnp.concatenate(
                [class_ref[pl.ds(first_row + j, 1), :] for j in range(2)], axis=1
            )
            low_class = lax.rem(classes, low_classes)
            high_class = classes // low_classes
            stacked = jnp.concatenate(
                [jnp.where(low_class == j, values, 0.0) for j in range(low_classes)], axis=0
            ).astype(jnp.bfloat16)
            products = jnp.dot(chunk_weights[b], stacked, preferred_element_type=jnp.float32)
            result = products[0:bins_all]
            for a in range(1, high_classes):
                result = jnp.where(
                    high_class == a, products[a * bins_all : (a + 1) * bins_all], result
                )
            if b > 0:
                result += sums[step]
            if b < half - 1:
                sums[step] = result
            else:
                for j in range(2):
                    out_ref[pl.ds(first_row + j, bins_all, stride=cells), :] = result[
                        :, j * grid_z : (j + 1) * grid_z
                    ]
            return carry

        lax.fori_loop(0, cells // 2, pair, 0, unroll=8)

    for copy in parms + swaps:
        copy.wait_send()
    for b in range(half):
        for s in range(2):
            halos[b][s].wait_send()
    for b in range(half):
        update(b)

    sent = rounded.at[:, pl.ds(0, ring - 1)]
    pltpu.make_async_copy(sent, sent, spread_send).wait()


def solution(mesh):
    gx_count, ba_count = mesh.shape["gx"], mesh.shape["ba"]

    def step(density, diffusivity, positions, spectrum, cell_class, operators):
        bins_dev, planes, rows_y, grid_z = density.shape
        classes, bins_all, _ = operators.shape
        remnants = positions.shape[0]
        half = bins_dev // 2
        cells = planes * (rows_y // ba_count)
        quad, low_classes = 4, 16
        vmem = pl.BlockSpec(memory_space=pltpu.VMEM)
        out = pl.pallas_call(
            functools.partial(kernel, gx_count, ba_count),
            out_shape=jax.ShapeDtypeStruct((bins_all * cells, grid_z), jnp.float32),
            in_specs=[pl.BlockSpec(memory_space=pltpu.HBM)] * 6,
            out_specs=vmem,
            scratch_shapes=[
                pltpu.SMEM((bins_dev,), jnp.float32),
                pltpu.VMEM((1, remnants), jnp.int32),
                pltpu.VMEM((bins_dev, remnants), jnp.float32),
                pltpu.VMEM((cells, grid_z), jnp.int32),
                pltpu.VMEM(density.shape, jnp.float32),
                pltpu.VMEM((2, half, planes, rows_y, grid_z), jnp.int16),
                pltpu.VMEM((2, half, planes, rows_y, grid_z), jnp.int16),
                pltpu.VMEM((2, half, planes, rows_y, grid_z), jnp.int16),
                pltpu.VMEM((2, half, remnants // 2 + grid_z), jnp.float32),
                pltpu.VMEM((2, half, remnants // 2 + grid_z), jnp.float32),
                pltpu.VMEM((half, 2 * planes + 2, rows_y, grid_z), jnp.float32),
                pltpu.VMEM((half, 2 * planes, rows_y, grid_z), jnp.float32),
                pltpu.VMEM((half, 2 * ba_count, cells, grid_z), jnp.bfloat16),
                pltpu.VMEM((half, 2 * ba_count, cells, grid_z), jnp.bfloat16),
                pltpu.VMEM((2 * ba_count * cells, grid_z), jnp.float32),
                pltpu.VMEM((cells // 2, bins_all, 2 * grid_z), jnp.float32),
                pltpu.VMEM(operators.shape, jnp.bfloat16),
                pltpu.VMEM((classes // quad * bins_all, quad * bins_all), jnp.bfloat16),
                pltpu.VMEM((half, classes // low_classes * bins_all, low_classes * 2 * ba_count), jnp.bfloat16),
                pltpu.SemaphoreType.DMA((5 + bins_dev,)),
                pltpu.SemaphoreType.DMA((2, half)),
                pltpu.SemaphoreType.DMA((2, half)),
                pltpu.SemaphoreType.DMA((2,)),
                pltpu.SemaphoreType.DMA((2,)),
                pltpu.SemaphoreType.DMA((2, half)),
                pltpu.SemaphoreType.DMA((2, half)),
                pltpu.SemaphoreType.DMA,
                pltpu.SemaphoreType.DMA((half,)),
            ],
            compiler_params=pltpu.CompilerParams(
                collective_id=0, has_side_effects=True, vmem_limit_bytes=16 * 2**20
            ),
        )(
            *[
                pltpu.with_memory_space_constraint(operand, pltpu.HBM)
                for operand in (
                    diffusivity,
                    density,
                    positions.reshape(1, remnants),
                    spectrum.T,
                    cell_class.reshape(cells, grid_z),
                    operators,
                )
            ]
        )
        return out.reshape(bins_all, planes, rows_y // ba_count, grid_z)

    in_specs = (P("ba", "gx", None, None), P("ba"), P(), P(None, "ba"), P("gx", "ba", None), P())
    return jax.shard_map(
        step, mesh=mesh, in_specs=in_specs, out_specs=P(None, "gx", "ba", None), check_vma=False
    )
```

```python
import functools

import jax
import jax.numpy as jnp
from jax import lax
from jax.experimental import pallas as pl
from jax.experimental.pallas import tpu as pltpu
from jax.sharding import PartitionSpec as P

MESH = pl.DeviceIdType.MESH

LOW = 0.1
STEPS = 32767.0
BIAS = 32768


def encode(rho):
    return ((rho - LOW) * STEPS + 0.5).astype(jnp.int32) - BIAS


def decode(code):
    return code.astype(jnp.int32).astype(jnp.float32) * (1.0 / STEPS) + (LOW + BIAS / STEPS)


def yz_sum(field):
    return (
        pltpu.roll(field, 1, 0)
        + pltpu.roll(field, field.shape[0] - 1, 0)
        + pltpu.roll(field, 1, 1)
        + pltpu.roll(field, field.shape[1] - 1, 1)
    )


def kernel(
    gx_count,
    ba_count,
    diff_hbm,
    density_ref,
    pos_hbm,
    spec_hbm,
    class_hbm,
    oper_ref,
    out_ref,
    diff_ref,
    pos_ref,
    spec_ref,
    class_ref,
    dens,
    stage,
    held,
    halo,
    parm_out,
    parm,
    source,
    inner,
    rounded,
    gathered,
    wide,
    sums,
    opers,
    weights,
    chunk_weights,
    load_sem,
    swap_send,
    swap_recv,
    parm_send,
    parm_recv,
    halo_send,
    halo_recv,
    spread_send,
    spread_recv,
):
    bins_dev, planes, rows_y, grid_z = density_ref.shape
    half = bins_dev // 2
    ring = 2 * ba_count
    rows_dev = rows_y // ba_count
    bins_all = opers.shape[1]
    remnants = pos_ref.shape[1]
    part = remnants // 2
    gx = lax.axis_index("gx")
    ba = lax.axis_index("ba")
    side = lax.rem(gx, 2)
    column = gx - side
    me = side * ba_count + ba
    meet = lax.rem(ba + ba_count // 2, ba_count)
    right = lax.rem(gx + 2, gx_count)
    left = lax.rem(gx + gx_count - 2, gx_count)

    barrier = pltpu.get_barrier_semaphore()
    greetings = 0
    for chips in (0, 1, 2, ring // 2 - 2, ring // 2 - 1):
        for core in range(2):
            if chips or core:
                peer = 2 * lax.rem(me // 2 + chips, ring // 2) + lax.rem(me + core, 2)
                pl.semaphore_signal(
                    barrier,
                    inc=1,
                    device_id=(column + peer // ba_count, lax.rem(peer, ba_count)),
                    device_id_type=MESH,
                )
                greetings += 1
    for other in (left, right):
        pl.semaphore_signal(barrier, inc=1, device_id=(other, ba), device_id_type=MESH)
        greetings += 1

    loads = [
        pltpu.make_async_copy(diff_hbm, diff_ref, load_sem.at[0]),
        pltpu.make_async_copy(spec_hbm, spec_ref, load_sem.at[1]),
        pltpu.make_async_copy(pos_hbm, pos_ref, load_sem.at[2]),
        pltpu.make_async_copy(oper_ref, opers, load_sem.at[3]),
        pltpu.make_async_copy(class_hbm, class_ref, load_sem.at[4]),
    ]
    loads += [
        pltpu.make_async_copy(
            density_ref.at[h * half + b], dens.at[h * half + b], load_sem.at[5 + h * half + b]
        )
        for b in range(half)
        for h in range(2)
    ]
    for copy in loads[:2] + loads[5:] + loads[2:5]:
        copy.start()

    loads[0].wait()
    loads[1].wait()
    bin_row = lax.broadcasted_iota(jnp.int32, (half, grid_z), 0)
    for h in range(2):
        parm_out[h, :, 0:part] = spec_ref[
            h * half : (h + 1) * half, pl.ds(pl.multiple_of(side * part, part), part)
        ]
        value = jnp.zeros((half, grid_z), jnp.float32)
        for b in range(half):
            value = jnp.where(bin_row == b, diff_ref[h * half + b], value)
        parm_out[h, :, part:] = value
    swaps = []

    def encode_chunk(b):
        for h in range(2):
            loads[5 + 2 * b + h].wait()
            stage[h, b] = encode(dens[h * half + b]).astype(jnp.int16)

    def swap(b):
        for h in range(2):
            swaps.append(
                pltpu.make_async_remote_copy(
                    src_ref=stage.at[h, b],
                    dst_ref=held.at[side, b],
                    send_sem=swap_send.at[h, b],
                    recv_sem=swap_recv.at[side, b],
                    device_id=(column + h, meet),
                    device_id_type=MESH,
                )
            )
            swaps[-1].start()

    encode_chunk(0)
    pl.semaphore_wait(barrier, greetings)

    parms = []
    for h in range(2):
        target = (column + h, meet)
        parms.append(
            pltpu.make_async_remote_copy(
                src_ref=parm_out.at[h],
                dst_ref=parm.at[side],
                send_sem=parm_send.at[h],
                recv_sem=parm_recv.at[side],
                device_id=target,
                device_id_type=MESH,
            )
        )
        parms[h].start()
    swap(0)
    for b in range(1, half):
        encode_chunk(b)

    loads[2].wait()
    loads[3].wait()
    loads[4].wait()
    quad = weights.shape[1] // bins_all
    quads = weights.shape[0] // bins_all
    swap(1)

    planes_col = 2 * planes
    planes_src = planes_col + 2
    pos = pos_ref[...]
    pos_x = pos // (rows_y * grid_z)
    pos_y = lax.rem(pos // grid_z, rows_y)
    pos_z = lax.rem(pos, grid_z)
    width = gx_count * planes
    pos_x = lax.rem(pos_x + (width + 1) - column * planes, width)
    pos_row = pos_x * rows_y + pos_y
    is_row = lax.broadcasted_iota(jnp.int32, (planes_src * rows_y, remnants), 0) == pos_row
    is_row = jnp.where(is_row, 1.0, 0.0).astype(jnp.bfloat16)
    is_z = lax.broadcasted_iota(jnp.int32, (grid_z, remnants), 0) == pos_z
    for s in range(2):
        pltpu.make_async_copy(parm.at[s], parm.at[s], parm_recv.at[s]).wait()
    swap(2)
    spec = jnp.concatenate([parm[0, :, 0:part], parm[1, :, 0:part]], axis=1)
    high = spec.astype(jnp.bfloat16).astype(jnp.float32)
    low = spec - high

    def inject(pair):
        total = jnp.zeros((planes_src * rows_y, 2 * grid_z), jnp.float32)
        for piece in (high, low):
            placed = [
                jnp.where(is_z, piece[b : b + 1], 0.0).astype(jnp.bfloat16)
                for b in (2 * pair, 2 * pair + 1)
            ]
            total += lax.dot_general(
                is_row,
                jnp.concatenate(placed, axis=0),
                (((1,), (1,)), ((), ())),
                preferred_element_type=jnp.float32,
            )
        for j in range(2):
            source[2 * pair + j] = total[:, j * grid_z : (j + 1) * grid_z].reshape(
                planes_src, rows_y, grid_z
            )

    halos = [[None, None] for _ in range(half)]

    def forward(b):
        for s in range(2):
            pltpu.make_async_copy(held.at[s, b], held.at[s, b], swap_recv.at[s, b]).wait()
            halos[b][s] = pltpu.make_async_remote_copy(
                src_ref=held.at[s, b],
                dst_ref=halo.at[s, b],
                send_sem=halo_send.at[s, b],
                recv_sem=halo_recv.at[s, b],
                device_id=(left if s == 0 else right, ba),
                device_id_type=MESH,
            )
            halos[b][s].start()

    low_classes = chunk_weights.shape[2] // ring
    high_classes = chunk_weights.shape[1] // bins_all

    def regroup():
        size = weights.shape[1]
        k = lax.broadcasted_iota(jnp.int32, (size, size), 0)
        n = lax.broadcasted_iota(jnp.int32, (size, size), 1)
        wanted = (n // bins_all) + half * lax.rem(n, ring)
        pick = (k // bins_all == lax.rem(n, bins_all) // ring) & (lax.rem(k, bins_all) == wanted)
        pick = jnp.where(pick, 1.0, 0.0).astype(jnp.bfloat16)
        per_high = low_classes // quad

        def one(a, carry):
            rows = pl.ds(pl.multiple_of(a * per_high * bins_all, bins_all), per_high * bins_all)
            picked = jnp.dot(weights[rows, :], pick, preferred_element_type=jnp.float32)
            picked = picked.astype(jnp.bfloat16)
            place = pl.ds(pl.multiple_of(a * bins_all, bins_all), bins_all)
            for b in range(half):
                chunk_weights[b, place, :] = jnp.concatenate(
                    [
                        picked[t * bins_all : (t + 1) * bins_all, b * bins_all : (b + 1) * bins_all]
                        for t in range(per_high)
                    ],
                    axis=1,
                )
            return carry

        lax.fori_loop(0, high_classes, one, 0)

    def prepare(b):
        rate = parm[0, b : b + 1, part:]
        centre = 1.0 - 6.0 * rate
        fields = [decode(held[s, b, p]) for s in range(2) for p in range(planes)]
        for p in range(planes_col):
            around = yz_sum(fields[p])
            if p > 0:
                around += fields[p - 1]
            if p + 1 < planes_col:
                around += fields[p + 1]
            inner[b, p] = centre * fields[p] + rate * around + source[b, p + 1]

    def diffuse(b):
        for s in range(2):
            halos[b][s].wait_recv()
        rate = parm[0, b : b + 1, part:]
        centre = 1.0 - 6.0 * rate
        before = [decode(halo[1, b, p]) for p in range(planes)]
        after = [decode(halo[0, b, p]) for p in range(planes)]
        sources = [source[b, p] for p in range(planes_src)]
        first = [
            centre * before[-1]
            + rate * (before[-2] + decode(held[0, b, 0]) + yz_sum(before[-1]))
            + sources[0]
        ]
        first += [inner[b, p] for p in range(planes_col)]
        first[1] += rate * before[-1]
        first[planes_col] += rate * after[0]
        first.append(
            centre * after[0]
            + rate * (decode(held[1, b, planes - 1]) + after[1] + yz_sum(after[0]))
            + sources[planes_src - 1]
        )
        second = [
            centre * first[p + 1]
            + rate * (first[p] + first[p + 2] + yz_sum(first[p + 1]))
            + sources[p + 1]
            for p in range(planes_col)
        ]
        for s in range(2):
            block = jnp.concatenate(
                [second[s * planes + p].reshape(ba_count, rows_dev, grid_z) for p in range(planes)],
                axis=1,
            )
            rounded[b, pl.ds(s * ba_count, ba_count)] = block.astype(jnp.bfloat16)

    group = 2 * meet + side
    peers = []
    for offset in sorted(range(1, ring), key=lambda o: -min(o, ring - o)):
        peer = lax.rem(me + offset, ring)
        peers.append((peer, (column + peer // ba_count, lax.rem(peer, ba_count))))

    def spread(b):
        slot = gathered.at[b, group]
        for peer, place in peers:
            pltpu.make_async_remote_copy(
                src_ref=rounded.at[b, peer],
                dst_ref=slot,
                send_sem=spread_send,
                recv_sem=spread_recv.at[b],
                device_id=place,
                device_id_type=MESH,
            ).start()
        pltpu.make_async_copy(rounded.at[b, me], slot, spread_recv.at[b]).start()

    inject(0)
    swap(3)
    forward(0)
    prepare(0)
    inject(1)
    forward(1)
    prepare(1)
    forward(2)
    prepare(2)
    forward(3)
    prepare(3)
    diffuse(0)
    spread(0)
    diffuse(1)
    spread(1)
    diffuse(2)
    spread(2)
    diffuse(3)
    spread(3)

    def arrange(a, carry):
        weights[pl.ds(pl.multiple_of(a * bins_all, bins_all), bins_all), :] = jnp.concatenate(
            [opers[a * quad + j] for j in range(quad)], axis=1
        )
        return carry

    lax.fori_loop(0, quads, arrange, 0, unroll=4)
    regroup()

    cells = planes * rows_dev

    def update(b):
        pltpu.make_async_copy(gathered.at[b], gathered.at[b], spread_recv.at[b]).wait()
        wide[...] = gathered[b].astype(jnp.float32).reshape(wide.shape)

        def pair(step, carry):
            first_row = 2 * step
            values = jnp.concatenate(
                [wide[pl.ds(first_row + j, ring, stride=cells), :] for j in range(2)], axis=1
            )
            classes = jnp.concatenate(
                [class_ref[pl.ds(first_row + j, 1), :] for j in range(2)], axis=1
            )
            low_class = lax.rem(classes, low_classes)
            high_class = classes // low_classes
            stacked = jnp.concatenate(
                [jnp.where(low_class == j, values, 0.0) for j in range(low_classes)], axis=0
            ).astype(jnp.bfloat16)
            products = jnp.dot(chunk_weights[b], stacked, preferred_element_type=jnp.float32)
            result = products[0:bins_all]
            for a in range(1, high_classes):
                result = jnp.where(
                    high_class == a, products[a * bins_all : (a + 1) * bins_all], result
                )
            if b > 0:
                result += sums[step]
            if b < half - 1:
                sums[step] = result
            else:
                for j in range(2):
                    out_ref[pl.ds(first_row + j, bins_all, stride=cells), :] = result[
                        :, j * grid_z : (j + 1) * grid_z
                    ]
            return carry

        lax.fori_loop(0, cells // 2, pair, 0, unroll=8)

    for b in range(half):
        update(b)

    for copy in parms + swaps:
        copy.wait_send()
    for b in range(half):
        for s in range(2):
            halos[b][s].wait_send()
    sent = rounded.at[:, pl.ds(0, ring - 1)]
    pltpu.make_async_copy(sent, sent, spread_send).wait()


def solution(mesh):
    gx_count, ba_count = mesh.shape["gx"], mesh.shape["ba"]

    def step(density, diffusivity, positions, spectrum, cell_class, operators):
        bins_dev, planes, rows_y, grid_z = density.shape
        classes, bins_all, _ = operators.shape
        remnants = positions.shape[0]
        half = bins_dev // 2
        cells = planes * (rows_y // ba_count)
        quad, low_classes = 4, 16
        vmem = pl.BlockSpec(memory_space=pltpu.VMEM)
        out = pl.pallas_call(
            functools.partial(kernel, gx_count, ba_count),
            out_shape=jax.ShapeDtypeStruct((bins_all * cells, grid_z), jnp.float32),
            in_specs=[pl.BlockSpec(memory_space=pltpu.HBM)] * 6,
            out_specs=vmem,
            scratch_shapes=[
                pltpu.SMEM((bins_dev,), jnp.float32),
                pltpu.VMEM((1, remnants), jnp.int32),
                pltpu.VMEM((bins_dev, remnants), jnp.float32),
                pltpu.VMEM((cells, grid_z), jnp.int32),
                pltpu.VMEM(density.shape, jnp.float32),
                pltpu.VMEM((2, half, planes, rows_y, grid_z), jnp.int16),
                pltpu.VMEM((2, half, planes, rows_y, grid_z), jnp.int16),
                pltpu.VMEM((2, half, planes, rows_y, grid_z), jnp.int16),
                pltpu.VMEM((2, half, remnants // 2 + grid_z), jnp.float32),
                pltpu.VMEM((2, half, remnants // 2 + grid_z), jnp.float32),
                pltpu.VMEM((half, 2 * planes + 2, rows_y, grid_z), jnp.float32),
                pltpu.VMEM((half, 2 * planes, rows_y, grid_z), jnp.float32),
                pltpu.VMEM((half, 2 * ba_count, cells, grid_z), jnp.bfloat16),
                pltpu.VMEM((half, 2 * ba_count, cells, grid_z), jnp.bfloat16),
                pltpu.VMEM((2 * ba_count * cells, grid_z), jnp.float32),
                pltpu.VMEM((cells // 2, bins_all, 2 * grid_z), jnp.float32),
                pltpu.VMEM(operators.shape, jnp.bfloat16),
                pltpu.VMEM((classes // quad * bins_all, quad * bins_all), jnp.bfloat16),
                pltpu.VMEM((half, classes // low_classes * bins_all, low_classes * 2 * ba_count), jnp.bfloat16),
                pltpu.SemaphoreType.DMA((5 + bins_dev,)),
                pltpu.SemaphoreType.DMA((2, half)),
                pltpu.SemaphoreType.DMA((2, half)),
                pltpu.SemaphoreType.DMA((2,)),
                pltpu.SemaphoreType.DMA((2,)),
                pltpu.SemaphoreType.DMA((2, half)),
                pltpu.SemaphoreType.DMA((2, half)),
                pltpu.SemaphoreType.DMA,
                pltpu.SemaphoreType.DMA((half,)),
            ],
            compiler_params=pltpu.CompilerParams(
                collective_id=0, has_side_effects=True, vmem_limit_bytes=16 * 2**20
            ),
        )(
            *[
                pltpu.with_memory_space_constraint(operand, pltpu.HBM)
                for operand in (
                    diffusivity,
                    density,
                    positions.reshape(1, remnants),
                    spectrum.T,
                    cell_class.reshape(cells, grid_z),
                    operators,
                )
            ]
        )
        return out.reshape(bins_all, planes, rows_y // ba_count, grid_z)

    in_specs = (P("ba", "gx", None, None), P("ba"), P(), P(None, "ba"), P("gx", "ba", None), P())
    return jax.shard_map(
        step, mesh=mesh, in_specs=in_specs, out_specs=P(None, "gx", "ba", None), check_vma=False
    )
```
